256 devices in a mesh: samp: 4 (over y), var: 64 (over x, z, core).
Axes of the slice: x: 4, y: 4, z: 8, core: 2. Of those that a mesh axis runs over, the one named last changes fastest.
Arguments:
- observed: bfloat16 [1024, 262144], P('samp', 'var'), may hold values from -6 to 6
- blocks: float32 [2048, 2, 128, 128], P('var'), may hold values from -6 to 6
- diagonal: float32 [262144], P('var'), may hold values from 1 to 4
- pattern: int32 [2048, 2], P('var'), may hold values from 0 to 2047, as said below
Outputs:
- new_blocks: float32 [2048, 2, 128, 128], P('var')
- new_diagonal: float32 [262144], P('var')
- objective: float32 [2], replicated
The draws below stay inside these ranges and needn't reach their ends.
Inputs may be any that keep to these rules, and one draw needn't show every extreme that they name: pattern[c, 0] and pattern[c, 1] are two different row-block indices, one of them equal to c. For each index v of var, among its block columns c = v * 32 to v * 32 + 31, for every u, at most 2 of the entries that differ from c name row blocks in the range u * 32 to u * 32 + 31, and for some u exactly 2 do.
All inputs are finite; a program needn't handle non-finite values.
Results may differ from the reference program's by a relative error of at most 0.0049.
Values may be sent and summed in bfloat16 or wider, within the bound.
No kernel may reach another device: no remote copies, remote signals or barrier semaphores. Data moves between devices by JAX's collectives and lax.ppermute only.
A program may use at most 128 MiB of HBM per device.

```python
import math
import jax
import jax.numpy as jnp
from jax import lax

BW = 128
CPD = 32
STEPS = 2
NBC = 2048
P_SIZE = 262144
SAMPLES = 1024
CAP = 2
N_VAR = 64


def draw_pattern(key, part):
    first_draw = jax.random.randint(jax.random.fold_in(key, 11), (N_VAR,), 0, N_VAR)
    second_draw = jax.random.randint(jax.random.fold_in(key, 12), (N_VAR,), 0, N_VAR)
    reorder_permutation = jax.random.permutation(jax.random.fold_in(key, 13), N_VAR)
    hot_owner = reorder_permutation[first_draw * second_draw // N_VAR]
    offset = jax.random.randint(jax.random.fold_in(key, 14), (N_VAR, 1), 0, N_VAR - 1)
    position = jnp.arange(CPD, dtype=jnp.int32)[None, :]
    spread = (hot_owner[:, None] + 1 + (position - CAP + offset) % (N_VAR - 1)) % N_VAR
    owners = jnp.where(position < CAP, hot_owner[:, None], spread)
    scores = jax.random.randint(jax.random.fold_in(key, 15), (N_VAR, CPD), 0, 1024) * CPD + position
    column_order = jnp.argsort(scores, axis=1)
    owners = jnp.take_along_axis(owners, column_order, axis=1)
    resident_index = jax.random.randint(jax.random.fold_in(key, 16), (N_VAR, CPD), 0, CPD)
    devices = jnp.arange(N_VAR, dtype=jnp.int32)[:, None]
    own_column = devices * CPD + position
    row_block = owners * CPD + resident_index
    row_block = jnp.where(row_block == own_column, owners * CPD + (resident_index + 1) % CPD, row_block)
    slot_flip = jax.random.randint(jax.random.fold_in(key, 17), (N_VAR, CPD), 0, 2)
    paired = jnp.where((slot_flip == 0)[:, :, None], jnp.stack([own_column, row_block], -1), jnp.stack([row_block, own_column], -1))
    return paired.reshape(NBC, 2).astype(jnp.int32)


def levels(own_key, shape, split, smallest, top_value):
    gain, own = 1.0, jax.random.fold_in(own_key, 6)
    for axis_at, blocks in split:
        draws = jnp.exp(jax.random.uniform(jax.random.fold_in(own, axis_at), (blocks,), jnp.float32, smallest / len(split), top_value / len(split)))
        gain = gain * jnp.repeat(draws, shape[axis_at] // blocks).reshape([-1 if axis == axis_at else 1 for axis in range(len(shape))])
    return gain


def bell_draw(stream_key, dims, scale, most, cuts=(), kind=jnp.bfloat16):
    array = scale * jax.random.normal(stream_key, dims, jnp.float32)
    if cuts:
        array = array * levels(stream_key, dims, cuts, -0.22, 0.18)
    return jnp.clip(array, -most, most).astype(kind)


def setup_inputs(seed: int = 0) -> dict:
    seeds = jax.random.split(jax.random.key(seed), 5)
    observed = bell_draw(seeds[0], (SAMPLES, P_SIZE), 1.0, 6.0, ((0, 4), (1, 64)))
    blocks = bell_draw(seeds[1], (NBC, 2, BW, BW), 1.0, 6.0, ((0, 64),), jnp.float32)
    diagonal = jnp.clip(jnp.exp(math.log(4.0) - 1.3862944 * jax.random.uniform(seeds[2], (P_SIZE,), jnp.float32) ** levels(seeds[2], (P_SIZE,), ((0, 64),), -0.2, 0.2)), 1.0, 4.0)
    pattern = draw_pattern(jax.random.fold_in(seeds[4], 71), 0)
    return {"observed": observed, "blocks": blocks, "diagonal": diagonal, "pattern": pattern}


step_length = 0.5
penalty = 0.5

def shrink(moved, level):
    return jnp.sign(moved) * jnp.maximum(jnp.abs(moved) - level, 0.0)

def reference(observed, blocks, diagonal, pattern):
    block_count = blocks.shape[0]
    block_width = blocks.shape[2]
    sample_count = observed.shape[0]
    matrix_order = block_count * block_width
    group_size = math.gcd(block_count, 64)
    group_count = block_count // group_size
    column_tiles = observed.reshape(sample_count, block_count, block_width)
    columns = jnp.arange(block_count, dtype=jnp.int32)
    on_diag = pattern == columns[:, None]
    diag_mask = jnp.eye(block_width, dtype=bool)
    element_mask = on_diag[:, :, None, None] & diag_mask
    stored = jnp.where(element_mask, jnp.float32(0.0), blocks)
    diag_values = diagonal.reshape(block_count, block_width)

    def column_group(inputs):
        pattern_group, block_group, value_group, flag_group = inputs
        picked = jnp.take(column_tiles, pattern_group.reshape(-1), axis=1)
        picked = picked.reshape(sample_count, group_size, 2, block_width).astype(jnp.float32)
        full_blocks = jnp.where(flag_group[:, :, None, None] & diag_mask, value_group[:, None, None, :], block_group)
        rounded = lax.optimization_barrier(full_blocks.astype(jnp.bfloat16)).astype(jnp.float32)
        product = jnp.einsum('sgkb,gkbn->sgn', picked, rounded, precision=lax.Precision.HIGHEST)
        squares = jnp.sum(product * product)
        lower_precision_product = lax.optimization_barrier(product.astype(jnp.bfloat16)).astype(jnp.float32)
        gradient = jnp.einsum('sgkb,sgn->gkbn', picked, lower_precision_product, precision=lax.Precision.HIGHEST)
        return (gradient, squares)
    objectives = []
    for iteration in range(STEPS):
        gradient, squares = lax.map(column_group, (pattern.reshape(group_count, group_size, 2), stored.reshape(group_count, group_size, 2, block_width, block_width), diag_values.reshape(group_count, group_size, block_width), on_diag.reshape(group_count, group_size, 2)))
        gradient = gradient.reshape(block_count, 2, block_width, block_width) / sample_count
        total = -jnp.sum(jnp.log(diag_values)) + jnp.sum(squares) / (2.0 * sample_count) + penalty * jnp.sum(jnp.abs(stored))
        objectives.append(total / matrix_order)
        moved = stored - step_length * gradient
        stored = jnp.where(element_mask, jnp.float32(0.0), shrink(moved, step_length * penalty))
        along = lax.optimization_barrier(jnp.sum(jnp.where(element_mask, gradient, jnp.float32(0.0)), axis=(1, 2)))
        moved_diag = diag_values - step_length * along
        diag_values = 0.5 * (moved_diag + jnp.sqrt(moved_diag * moved_diag + 4.0 * step_length))
    return (stored, diag_values.reshape(-1), jnp.stack(objectives))
```

```python
import functools

import jax
import jax.numpy as jnp
from jax import lax
from jax.experimental import pallas as pl
from jax.experimental.pallas import tpu as pltpu
from jax.sharding import Mesh
from jax.sharding import PartitionSpec as P

STEPS = 2
STEP_LENGTH = 0.5
PENALTY = 0.5
VAR = ("var_0", "var_1", "var_2")
ALL = ("samp", "var_0", "var_1", "var_2")
F32 = jnp.float32
BF16 = jnp.bfloat16


def shifts(x, axis, which):
    n = lax.axis_size(axis)
    return [lax.ppermute(x, axis, [(i, (i + k) % n) for i in range(n)]) for k in which]


def everyones(x, axes):
    for axis in axes:
        x = jnp.stack([x] + shifts(x, axis, range(1, lax.axis_size(axis))))
    return x


def pick_kernel(sizes, cols, at_ref, wanted_ref, table_ref, out_ref):
    n0, n1, n2 = sizes
    share = pl.program_id(0)

    @pl.loop(0, n0 * n1 * n2)
    def _(d):
        k0 = lax.rem(at_ref[0] - d // (n1 * n2) + n0, n0)
        k1 = lax.rem(at_ref[1] - lax.rem(d // n2, n1) + n1, n1)
        k2 = lax.rem(at_ref[2] - lax.rem(d, n2) + n2, n2)
        row = ((k0 * n2 + k2) * n1 + k1) * cols + share * out_ref.shape[1]
        for j in range(out_ref.shape[1]):
            out_ref[d, j] = table_ref[wanted_ref[row + j]]


def pick(wanted, table, sizes, cols, shares):
    devices = sizes[0] * sizes[1] * sizes[2]
    each = cols // shares
    at = jnp.stack([lax.axis_index(a) for a in VAR]).astype(jnp.int32)
    piece = table.shape[1:]
    return pl.pallas_call(
        functools.partial(pick_kernel, sizes, cols),
        grid_spec=pltpu.PrefetchScalarGridSpec(
            num_scalar_prefetch=2,
            grid=(shares,),
            in_specs=[pl.BlockSpec(table.shape, lambda i, a, w: (0, 0, 0))],
            out_specs=pl.BlockSpec((devices, each) + piece, lambda i, a, w: (i, 0, 0, 0)),
        ),
        out_shape=jax.ShapeDtypeStruct((shares * devices, each) + piece, table.dtype),
        compiler_params=pltpu.CompilerParams(vmem_limit_bytes=32 << 20),
    )(at, wanted, table)


def shrink(v, level):
    return jnp.where(v > level, v - level, jnp.where(v < -level, v + level, 0.0))


def split3(g):
    hi = g.astype(BF16)
    rest = g - hi.astype(F32)
    mid = rest.astype(BF16)
    return hi, mid, (rest - mid.astype(F32)).astype(BF16)


def steps_kernel(total_rows, info_ref, own_ref, p1_ref, p2_ref, p3_ref, far_ref, blocks_ref, diag_ref,
                 out_ref, new_diag_ref, obj_ref):
    j = pl.program_id(0)
    samp = info_ref[0]
    rows = own_ref.shape[0]
    gram = None
    for k, near_ref in enumerate((own_ref, p1_ref, p2_ref, p3_ref)):
        q = lax.rem(samp + 4 - k, 4)
        far = far_ref[0, pl.ds(pl.multiple_of(q * rows, rows), rows), :]
        x = jnp.concatenate([near_ref[...], far], axis=1)
        term = lax.dot_general(x, x, (((0,), (0,)), ((), ())), preferred_element_type=F32)
        gram = term if gram is None else gram + term
    parts = split3(gram)
    width = out_ref.shape[-1]
    eye = lax.broadcasted_iota(jnp.int32, (width, width), 0) == lax.broadcasted_iota(jnp.int32, (width, width), 1)
    where_diag = info_ref[2 + j]
    db = jnp.where(eye, 0.0, blocks_ref[0, where_diag])
    ob = blocks_ref[0, 1 - where_diag]
    dv = diag_ref[pl.ds(j, 1), :]
    objs = []
    for _ in range(STEPS):
        full = jnp.where(eye, jnp.broadcast_to(dv, (width, width)), db)
        w = jnp.concatenate([full, ob], axis=0).astype(BF16)
        g = sum(jnp.dot(p, w, preferred_element_type=F32) for p in reversed(parts))
        part = jnp.sum(w.astype(F32) * g, axis=0, keepdims=True) / (2.0 * total_rows)
        part = part - jnp.log(dv)
        part = part + PENALTY * (jnp.sum(jnp.abs(db), axis=0, keepdims=True) + jnp.sum(jnp.abs(ob), axis=0, keepdims=True))
        objs.append(part)
        g = g / total_rows
        gd, go = g[:width], g[width:]
        along = jnp.sum(jnp.where(eye, gd, 0.0), axis=0, keepdims=True)
        db = jnp.where(eye, 0.0, shrink(db - STEP_LENGTH * gd, STEP_LENGTH * PENALTY))
        ob = shrink(ob - STEP_LENGTH * go, STEP_LENGTH * PENALTY)
        m = dv - STEP_LENGTH * along
        dv = 0.5 * (m + jnp.sqrt(m * m + 4.0 * STEP_LENGTH))
    out_ref[0, where_diag] = db.astype(out_ref.dtype)
    out_ref[0, 1 - where_diag] = ob.astype(out_ref.dtype)
    new_diag_ref[pl.ds(j, 1), :] = dv

    @pl.when(j == 0)
    def _():
        obj_ref[...] = jnp.zeros_like(obj_ref)

    for i, part in enumerate(objs):
        obj_ref[i : i + 1, :] += part


def iterate(info, observed, received, far, blocks, diag_rows, total_rows):
    rows = observed.shape[0]
    each, width = diag_rows.shape
    near = pl.BlockSpec((rows, width), lambda j, f: (0, j))
    return pl.pallas_call(
        functools.partial(steps_kernel, total_rows),
        grid_spec=pltpu.PrefetchScalarGridSpec(
            num_scalar_prefetch=1,
            grid=(each,),
            in_specs=[
                pl.BlockSpec((rows, width), lambda j, f: (0, f[1] + j)),
                near,
                near,
                near,
                pl.BlockSpec((1, far.shape[1], width), lambda j, f: (j, 0, 0)),
                pl.BlockSpec((1, 2, width, width), lambda j, f: (f[1] + j, 0, 0, 0)),
                pl.BlockSpec((each, width), lambda j, f: (0, 0)),
            ],
            out_specs=[
                pl.BlockSpec((1, 2, width, width), lambda j, f: (j, 0, 0, 0)),
                pl.BlockSpec((each, width), lambda j, f: (0, 0)),
                pl.BlockSpec((8, width), lambda j, f: (0, 0)),
            ],
        ),
        out_shape=[
            jax.ShapeDtypeStruct((each, 2, width, width), BF16),
            jax.ShapeDtypeStruct((each, width), F32),
            jax.ShapeDtypeStruct((8, width), F32),
        ],
        compiler_params=pltpu.CompilerParams(vmem_limit_bytes=32 << 20),
    )(info, observed, *received, far, blocks, diag_rows)


def place_kernel(samp_ref, own_ref, p1_ref, p2a_ref, p2b_ref, p3_ref, out_ref):
    samp, half = samp_ref[0], pl.num_programs(0) // 2
    out_ref[samp, 0] = own_ref[0].astype(F32)
    out_ref[lax.rem(samp + 3, 4), 0] = p1_ref[0].astype(F32)
    out_ref[lax.rem(samp + 1, 4), 0] = p3_ref[0].astype(F32)

    @pl.when(pl.program_id(0) < half)
    def _():
        out_ref[lax.rem(samp + 2, 4), 0] = p2a_ref[0].astype(F32)

    @pl.when(pl.program_id(0) >= half)
    def _():
        out_ref[lax.rem(samp + 2, 4), 0] = p2b_ref[0].astype(F32)


def gather_blocks(new, samp):
    each, tail = new.shape[0], new.shape[1:]
    half = each // 2
    (p1,) = shifts(new, "samp", (1,))
    (p3,) = shifts(new, "samp", (3,))
    (p2a,) = shifts(p1[:half], "samp", (1,))
    (p2b,) = shifts(p3[half:], "samp", (3,))
    zeros = (0,) * len(tail)
    whole = pl.BlockSpec((1,) + tail, lambda j, f: (j,) + zeros)
    out = pl.pallas_call(
        place_kernel,
        grid_spec=pltpu.PrefetchScalarGridSpec(
            num_scalar_prefetch=1,
            grid=(each,),
            in_specs=[
                whole,
                whole,
                pl.BlockSpec((1,) + tail, lambda j, f: (jnp.minimum(j, half - 1),) + zeros),
                pl.BlockSpec((1,) + tail, lambda j, f: (jnp.maximum(j - half, 0),) + zeros),
                whole,
            ],
            out_specs=pl.BlockSpec((4, 1) + tail, lambda j, f: (0, j) + zeros),
        ),
        out_shape=jax.ShapeDtypeStruct((4, each) + tail, F32),
        compiler_params=pltpu.CompilerParams(vmem_limit_bytes=32 << 20),
    )(samp[None], new, p1, p2a, p2b, p3)
    return out.reshape((4 * each,) + tail)


def body(observed, blocks, diagonal, pattern):
    cols, _, width, _ = blocks.shape
    rows = observed.shape[0]
    sizes = tuple(lax.axis_size(a) for a in VAR)
    devices = sizes[0] * sizes[1] * sizes[2]
    shares = lax.axis_size("samp")
    each = cols // shares
    piece_rows = rows // devices
    total_rows = rows * shares
    samp = lax.axis_index("samp").astype(jnp.int32)
    columns = lax.axis_index(VAR) * cols + jnp.arange(cols, dtype=jnp.int32)
    on_diag = pattern == columns[:, None]
    off_row = jnp.where(on_diag[:, 0], pattern[:, 1], pattern[:, 0])

    received = [
        shifts(lax.dynamic_slice_in_dim(observed, lax.rem(samp + k, shares) * each * width, each * width, 1), "samp", (k,))[0]
        for k in (1, 2, 3)
    ]
    pieces = observed.reshape(devices, piece_rows, cols, width).transpose(0, 2, 1, 3)
    table = lax.all_to_all(pieces, VAR, split_axis=0, concat_axis=0, tiled=True)
    wanted = everyones(off_row, ("var_1", "var_2", "var_0"))
    outgoing = pick(wanted.reshape(-1), table.reshape(devices * cols, piece_rows, width), sizes, cols, shares)
    far = lax.all_to_all(outgoing, ALL, split_axis=0, concat_axis=0, tiled=True)
    far = far.transpose(1, 0, 2, 3).reshape(each, total_rows, width)

    start = samp * each
    which = jnp.where(on_diag[:, 0], 0, 1).astype(jnp.int32)
    info = jnp.concatenate([jnp.stack([samp, start]), lax.dynamic_slice_in_dim(which, start, each, 0)])
    diag_rows = lax.dynamic_slice_in_dim(diagonal.reshape(cols, width), start, each, 0)
    new, new_diag, obj = iterate(info, observed, received, far, blocks, diag_rows, total_rows)

    new_blocks = gather_blocks(new, samp)
    near_diags = [new_diag] + shifts(new_diag, "samp", (1, 2, 3))
    order = [jnp.where(samp == q, near_diags[0], jnp.where(lax.rem(samp + 3, 4) == q, near_diags[1], jnp.where(lax.rem(samp + 2, 4) == q, near_diags[2], near_diags[3]))) for q in range(4)]
    new_diagonal = jnp.stack(order).reshape(-1)
    objective = jnp.sum(obj[:STEPS], axis=1) / (cols * devices * width)
    objective = functools.reduce(lax.psum, ALL, objective)
    return (new_blocks, new_diagonal, objective)


def solution(mesh):
    torus = Mesh(mesh.devices.reshape(mesh.shape["samp"], 4, 8, 2), ALL)
    placed = (P("samp", VAR), P(VAR, None, None, None), P(VAR), P(VAR, None))
    return jax.shard_map(
        body,
        mesh=torus,
        in_specs=placed,
        out_specs=(P(VAR, None, None, None), P(VAR), P()),
        check_vma=False,
    )
```

```python
import functools

import jax
import jax.numpy as jnp
from jax import lax
from jax.experimental import pallas as pl
from jax.experimental.pallas import tpu as pltpu
from jax.sharding import Mesh
from jax.sharding import PartitionSpec as P

STEPS = 2
STEP_LENGTH = 0.5
PENALTY = 0.5
DIGIT = 64
HALVES = 2
VAR = ("var_0", "var_1", "var_2")
ALL = ("samp", "var_0", "var_1", "var_2")
F32 = jnp.float32
BF16 = jnp.bfloat16
VMEM = pl.BlockSpec(memory_space=pltpu.VMEM)
ANY = pl.BlockSpec(memory_space=pl.ANY)
HBM = pl.BlockSpec(memory_space=pltpu.HBM)


def params(mib):
    return pltpu.CompilerParams(vmem_limit_bytes=mib << 20)


def cost(flops, bytes_accessed):
    return pl.CostEstimate(flops=flops, bytes_accessed=bytes_accessed, transcendentals=0)


def shift(x, axis, k):
    n = lax.axis_size(axis)
    return lax.ppermute(x, axis, [(i, (i + k) % n) for i in range(n)])


def cut_kernel(cols, at_ref, pattern_ref, data_ref, out_ref, note):
    width = note.shape[1]

    @pl.when(pl.program_id(0) == 0)
    def _():
        lane = lax.broadcasted_iota(jnp.int32, note.shape, 1)
        row = lax.broadcasted_iota(jnp.int32, note.shape, 0)
        digits = jnp.zeros(note.shape, jnp.int32)
        for k in range(cols):
            first, second = pattern_ref[2 * k], pattern_ref[2 * k + 1]
            block = jnp.where(first == at_ref[0] * cols + k, second, first)
            place = block + lax.div(block, cols)
            digit = jnp.where(row == 0, lax.div(place, DIGIT), lax.rem(place, DIGIT))
            digits = jnp.where(lane == k, digit, digits)
        note[...] = digits.astype(F32)

    wanted = note[...].astype(BF16)
    pieces, rows = out_ref.shape[0], out_ref.shape[2]
    for b in range(cols):
        tile = data_ref[:, b * width : (b + 1) * width]
        for i in range(pieces):
            out_ref[i, b] = tile[i * rows : (i + 1) * rows]
    for i in range(pieces):
        out_ref[i, cols] = wanted[:rows]


def cut(var_index, pattern, data, devices, cols, width):
    rows = data.shape[0] // devices
    pieces = 8
    return pl.pallas_call(
        functools.partial(cut_kernel, cols),
        grid_spec=pltpu.PrefetchScalarGridSpec(
            num_scalar_prefetch=2,
            grid=(devices // pieces,),
            in_specs=[pl.BlockSpec((pieces * rows, cols * width), lambda i, a, p: (i, 0))],
            out_specs=pl.BlockSpec((pieces, cols + 1, rows, width), lambda i, a, p: (i, 0, 0, 0)),
            scratch_shapes=[pltpu.VMEM((8, width), F32)],
        ),
        out_shape=jax.ShapeDtypeStruct((devices, cols + 1, rows, width), data.dtype),
        compiler_params=params(56),
    )(var_index[None], pattern.reshape(-1), data)


def pick_kernel(cols, shares, table_ref, *rest):
    out_ref, digits, wanted, held, sem, sems = rest[-6:]
    devices = digits.shape[0]
    each = cols // shares
    for u in range(devices):
        note = table_ref[u * (cols + 1) + cols].astype(F32)
        digits[u : u + 1, :] = (note[:1] * DIGIT + note[1:2]).astype(jnp.int32)
    move = pltpu.make_async_copy(digits, wanted, sem)
    move.start()
    move.wait()
    sent = []
    for s in range(shares):

        @pl.loop(0, devices, unroll=4)
        def _(d):
            for j in range(each):
                held[s, d, j] = table_ref[wanted[d, s * each + j]]

        copy = pltpu.make_async_copy(held.at[s], out_ref.at[pl.ds(s * devices, devices)], sems.at[s])
        copy.start()
        sent.append(copy)
    for copy in sent:
        copy.wait()


def pick(table, cols, shares, after):
    devices, _, rows, width = table.shape
    each = cols // shares
    return pl.pallas_call(
        functools.partial(pick_kernel, cols, shares),
        in_specs=[VMEM] + [HBM] * len(after),
        out_specs=HBM,
        out_shape=jax.ShapeDtypeStruct((shares * devices, each, rows, width), table.dtype),
        scratch_shapes=[
            pltpu.VMEM((devices, width), jnp.int32),
            pltpu.SMEM((devices, width), jnp.int32),
            pltpu.VMEM((shares, devices, each, rows, width), table.dtype),
            pltpu.SemaphoreType.DMA(()),
            pltpu.SemaphoreType.DMA((shares,)),
        ],
        compiler_params=params(56),
    )(table.reshape((devices * (cols + 1), rows, width)), *after)


def near_kernel(info_ref, own_ref, p1_ref, p2_ref, p3_ref, blocks_ref, near_ref, turned_ref, start_ref):
    samp, rows, width = info_ref[0], own_ref.shape[0], own_ref.shape[1]
    for k, ref in enumerate((own_ref, p1_ref, p2_ref, p3_ref)):
        q = lax.rem(samp + 4 - k, 4)
        at = pl.multiple_of(q * rows, rows)
        x = ref[...]
        near_ref[0, pl.ds(at, rows), :] = x
        turned_ref[0, :, pl.ds(at, rows)] = x.T
    where_diag = info_ref[2 + pl.program_id(0)]
    start_ref[0, :width] = blocks_ref[0, where_diag]
    start_ref[0, width:] = blocks_ref[0, 1 - where_diag]


def near_panels(info, observed, received, blocks, each):
    rows, width = observed.shape[0], blocks.shape[-1]
    part = pl.BlockSpec((rows, width), lambda j, f: (0, j))
    return pl.pallas_call(
        near_kernel,
        grid_spec=pltpu.PrefetchScalarGridSpec(
            num_scalar_prefetch=1,
            grid=(each,),
            in_specs=[
                pl.BlockSpec((rows, width), lambda j, f: (0, f[1] + j)),
                part,
                part,
                part,
                pl.BlockSpec((1, 2, width, width), lambda j, f: (f[1] + j, 0, 0, 0)),
            ],
            out_specs=[
                pl.BlockSpec((1, 4 * rows, width), lambda j, f: (j, 0, 0)),
                pl.BlockSpec((1, width, 4 * rows), lambda j, f: (j, 0, 0)),
                pl.BlockSpec((1, 2 * width, width), lambda j, f: (j, 0, 0)),
            ],
        ),
        out_shape=[
            jax.ShapeDtypeStruct((each, 4 * rows, width), BF16),
            jax.ShapeDtypeStruct((each, width, 4 * rows), BF16),
            jax.ShapeDtypeStruct((each, 2 * width, width), F32),
        ],
        compiler_params=params(56),
        cost_estimate=cost(1 << 20, 10 << 20),
    )(info, observed, *received, blocks)


def shrink(v, level):
    return jnp.where(v > level, v - level, jnp.where(v < -level, v + level, 0.0))


def split3(g):
    hi = g.astype(BF16)
    rest = g - hi.astype(F32)
    mid = rest.astype(BF16)
    return hi, mid, (rest - mid.astype(F32)).astype(BF16)


def steps_kernel(first, info_ref, far_ref, near_ref, turned_ref, start_ref, diag_ref, out_ref, new_diag_ref, obj_ref):
    count, total_rows, width = near_ref.shape
    step = pl.program_id(0)
    eye = lax.broadcasted_iota(jnp.int32, (width, width), 0) == lax.broadcasted_iota(jnp.int32, (width, width), 1)
    objs = [jnp.zeros((1, width), F32) for _ in range(STEPS)]
    for c in range(count):
        j = first + step * count + c
        far = far_ref[c]
        both = jnp.concatenate([near_ref[c], far], axis=1)
        top = jnp.dot(turned_ref[c], both, preferred_element_type=F32)
        low = lax.dot_general(far, both, (((0,), (0,)), ((), ())), preferred_element_type=F32)
        parts = split3(jnp.concatenate([top, low], axis=0))
        db = jnp.where(eye, 0.0, start_ref[c, :width])
        ob = start_ref[c, width:]
        dv = diag_ref[pl.ds(info_ref[1] + j, 1), :]
        for i in range(STEPS):
            full = jnp.where(eye, jnp.broadcast_to(dv, (width, width)), db)
            w = jnp.concatenate([full, ob], axis=0).astype(BF16)
            g = sum(jnp.dot(p, w, preferred_element_type=F32) for p in reversed(parts))
            fit = jnp.sum(w.astype(F32) * g, axis=0, keepdims=True) / (2.0 * total_rows)
            size = jnp.sum(jnp.abs(db) + jnp.abs(ob), axis=0, keepdims=True)
            objs[i] = objs[i] + (fit - jnp.log(dv) + PENALTY * size)
            g = g / total_rows
            gd, go = g[:width], g[width:]
            along = jnp.sum(jnp.where(eye, gd, 0.0), axis=0, keepdims=True)
            db = jnp.where(eye, 0.0, shrink(db - STEP_LENGTH * gd, STEP_LENGTH * PENALTY))
            ob = shrink(ob - STEP_LENGTH * go, STEP_LENGTH * PENALTY)
            m = dv - STEP_LENGTH * along
            dv = 0.5 * (m + jnp.sqrt(m * m + 4.0 * STEP_LENGTH))
        where_diag = info_ref[2 + j]
        out_ref[c, where_diag] = db.astype(out_ref.dtype)
        out_ref[c, 1 - where_diag] = ob.astype(out_ref.dtype)
        new_diag_ref[pl.ds(step * count + c, 1), :] = dv
    lane = lax.broadcasted_iota(jnp.int32, (1, width), 1)
    total = jnp.zeros((1, width), F32)
    for i in range(STEPS):
        total = jnp.where(lane == i, jnp.sum(objs[i], axis=1, keepdims=True), total)

    @pl.when(step == 0)
    def _():
        obj_ref[...] = total

    @pl.when(step > 0)
    def _():
        obj_ref[...] += total


def iterate(first, info, far, near, turned, start, diag_rows):
    count, total_rows, width = far.shape
    block = 2

    def columns(shape, offset):
        return pl.BlockSpec((block,) + shape, lambda i, f: (offset // block + i, 0, 0))

    return pl.pallas_call(
        functools.partial(steps_kernel, first),
        grid_spec=pltpu.PrefetchScalarGridSpec(
            num_scalar_prefetch=1,
            grid=(count // block,),
            in_specs=[
                columns((total_rows, width), 0),
                columns((total_rows, width), first),
                columns((width, total_rows), first),
                columns((2 * width, width), first),
                pl.BlockSpec(diag_rows.shape, lambda i, f: (0, 0)),
            ],
            out_specs=[
                pl.BlockSpec((block, 2, width, width), lambda i, f: (i, 0, 0, 0)),
                pl.BlockSpec((count, width), lambda i, f: (0, 0)),
                pl.BlockSpec((1, width), lambda i, f: (0, 0)),
            ],
        ),
        out_shape=[
            jax.ShapeDtypeStruct((count, 2, width, width), BF16),
            jax.ShapeDtypeStruct((count, width), F32),
            jax.ShapeDtypeStruct((1, width), F32),
        ],
        compiler_params=params(40),
        cost_estimate=cost(count << 29, 4 << 20),
    )(info, far, near, turned, start, diag_rows)


def first_places_kernel(samp_ref, h00, h01, h10, h11, h30, h31, out_ref):
    samp = samp_ref[0]
    for k, refs in ((0, (h00, h01)), (1, (h10, h11)), (3, (h30, h31))):
        q = lax.rem(samp + 4 - k, 4)
        for h, ref in enumerate(refs):
            out_ref[q, h, 0] = ref[0].astype(F32)


def last_places_kernel(samp_ref, h20, h21, _, out_ref):
    out_ref[0, 0, 0] = h20[0].astype(F32)
    out_ref[0, 1, 0] = h21[0].astype(F32)


def place_blocks(samp, own, one, three, two):
    count, tail = own[0].shape[0], own[0].shape[1:]
    zeros = (0,) * len(tail)
    part = pl.BlockSpec((1,) + tail, lambda j, f: (j,) + zeros)
    shape = jax.ShapeDtypeStruct((4, HALVES, count) + tail, F32)
    out = pl.pallas_call(
        first_places_kernel,
        grid_spec=pltpu.PrefetchScalarGridSpec(
            num_scalar_prefetch=1,
            grid=(count,),
            in_specs=[part] * 6,
            out_specs=pl.BlockSpec((4, HALVES, 1) + tail, lambda j, f: (0, 0, j) + zeros),
        ),
        out_shape=shape,
        compiler_params=params(24),
        cost_estimate=cost(1 << 20, 6 << 20),
    )(samp[None], *own, *one, *three)
    out = pl.pallas_call(
        last_places_kernel,
        grid_spec=pltpu.PrefetchScalarGridSpec(
            num_scalar_prefetch=1,
            grid=(count,),
            in_specs=[part, part, ANY],
            out_specs=pl.BlockSpec((1, HALVES, 1) + tail, lambda j, f: (lax.rem(f[0] + 2, 4), 0, j) + zeros),
        ),
        out_shape=shape,
        input_output_aliases={3: 0},
        compiler_params=params(16),
        cost_estimate=cost(1 << 20, 2 << 20),
    )(samp[None], *two, out)
    return out.reshape((4 * HALVES * count,) + tail)


def body(observed, blocks, diagonal, pattern):
    cols, _, width, _ = blocks.shape
    rows = observed.shape[0]
    devices = lax.axis_size(VAR)
    shares = lax.axis_size("samp")
    each = cols // shares
    half = each // HALVES
    total_rows = rows * shares
    samp = lax.axis_index("samp").astype(jnp.int32)
    var_index = lax.axis_index(VAR).astype(jnp.int32)

    pieces = cut(var_index, pattern, observed, devices, cols, width)
    panel = each * width
    received = [shift(lax.dynamic_slice_in_dim(observed, lax.rem(samp + k, shares) * panel, panel, 1), "samp", k) for k in (1, 2, 3)]
    table = lax.all_to_all(pieces, VAR, split_axis=0, concat_axis=0, tiled=True)
    start = samp * each
    columns = var_index * cols + jnp.arange(cols, dtype=jnp.int32)
    which = jnp.where(pattern[:, 0] == columns, 0, 1).astype(jnp.int32)
    info = jnp.concatenate([jnp.stack([samp, start]), lax.dynamic_slice_in_dim(which, start, each, 0)])
    near, turned, begin = near_panels(info, observed, received, blocks, each)
    outgoing = pick(table, cols, shares, (near, turned, begin))
    far = lax.all_to_all(outgoing, ALL, split_axis=0, concat_axis=0, tiled=True)

    diag_rows = diagonal.reshape(cols, width)
    new, diags, objs = [], [], []
    for h in range(HALVES):
        far_h = far[:, h * half : (h + 1) * half].transpose(1, 0, 2, 3).reshape(half, total_rows, width)
        done = iterate(h * half, info, far_h, near, turned, begin, diag_rows)
        new.append(done[0])
        diags.append(done[1])
        objs.append(done[2])

    one = [shift(x, "samp", 1) for x in new]
    three = [shift(x, "samp", 3) for x in new]
    two = [shift(one[0], "samp", 1), shift(three[1], "samp", 3)]
    new_blocks = place_blocks(samp, new, one, three, two)

    new_diag = jnp.concatenate(diags, axis=0)
    before = [new_diag] + [shift(new_diag, "samp", k) for k in (1, 2, 3)]
    order = []
    for q in range(4):
        k = lax.rem(samp + 4 - q, 4)
        order.append(jnp.where(k == 0, before[0], jnp.where(k == 1, before[1], jnp.where(k == 2, before[2], before[3]))))
    new_diagonal = jnp.stack(order).reshape(-1)

    mine = jnp.broadcast_to(objs[0] + objs[1], (shares * devices, width))
    objective = jnp.sum(lax.all_to_all(mine, ALL, split_axis=0, concat_axis=0, tiled=True), axis=0)
    return (new_blocks, new_diagonal, objective[:STEPS] / (cols * devices * width))


def solution(mesh):
    torus = Mesh(mesh.devices.reshape(mesh.shape["samp"], 4, 8, 2), ALL)
    placed = (P("samp", VAR), P(VAR, None, None, None), P(VAR), P(VAR, None))
    return jax.shard_map(
        body,
        mesh=torus,
        in_specs=placed,
        out_specs=(P(VAR, None, None, None), P(VAR), P()),
        check_vma=False,
    )
```

```python
import functools

import jax
import jax.numpy as jnp
from jax import lax
from jax.experimental import pallas as pl
from jax.experimental.pallas import tpu as pltpu
from jax.sharding import Mesh
from jax.sharding import PartitionSpec as P

STEPS = 2
STEP_LENGTH = 0.5
PENALTY = 0.5
DIGIT = 64
HALVES = 2
VAR = ("var_0", "var_1", "var_2")
ALL = ("samp", "var_0", "var_1", "var_2")
F32 = jnp.float32
BF16 = jnp.bfloat16
VMEM = pl.BlockSpec(memory_space=pltpu.VMEM)
ANY = pl.BlockSpec(memory_space=pl.ANY)
HBM = pl.BlockSpec(memory_space=pltpu.HBM)


def params(mib):
    return pltpu.CompilerParams(vmem_limit_bytes=mib << 20)


def cost(flops, bytes_accessed):
    return pl.CostEstimate(flops=flops, bytes_accessed=bytes_accessed, transcendentals=0)


def shift(x, axis, k):
    n = lax.axis_size(axis)
    return lax.ppermute(x, axis, [(i, (i + k) % n) for i in range(n)])


def cut_kernel(cols, at_ref, pattern_ref, data_ref, out_ref, note, sems):
    copies = [
        pltpu.make_async_copy(data_ref.at[:, :, h], out_ref.at[:, h, pl.ds(0, cols)], sems.at[h])
        for h in range(data_ref.shape[2])
    ]
    for copy in copies:
        copy.start()
    first, second = pattern_ref[0:1, :], pattern_ref[1:2, :]
    lane = lax.broadcasted_iota(jnp.int32, first.shape, 1)
    block = jnp.where(first == at_ref[0] * cols + lane, second, first)
    place = block + lax.div(block, cols)
    digits = jnp.concatenate([lax.div(place, DIGIT), lax.rem(place, DIGIT)], axis=0).astype(F32)
    rows, width = note.shape[-2:]
    wide = jnp.concatenate([digits, jnp.zeros((rows - 2, cols), F32)], axis=0)
    wide = jnp.concatenate([wide, jnp.zeros((rows, width - cols), F32)], axis=1).astype(note.dtype)
    note[...] = jnp.broadcast_to(wide, note.shape)
    tell = pltpu.make_async_copy(note, out_ref.at[:, :, pl.ds(cols, 1)], sems.at[len(copies)])
    tell.start()
    for copy in copies + [tell]:
        copy.wait()


def cut(var_index, pattern, data, devices, cols, width):
    rows = data.shape[0] // devices
    tile = 2 * rows
    view = data.reshape(devices // 2, tile, cols, width).transpose(0, 2, 1, 3).reshape(devices // 2, cols, 2, rows, width)
    out = pl.pallas_call(
        functools.partial(cut_kernel, cols),
        in_specs=[pl.BlockSpec(memory_space=pltpu.SMEM), VMEM, HBM],
        out_specs=HBM,
        out_shape=jax.ShapeDtypeStruct((devices // 2, 2, cols + 1, rows, width), data.dtype),
        scratch_shapes=[pltpu.VMEM((devices // 2, 2, 1, rows, width), data.dtype), pltpu.SemaphoreType.DMA((3,))],
        compiler_params=params(56),
    )(var_index[None], pattern.T, view)
    return out.reshape(devices, cols + 1, rows, width)


def pick_kernel(cols, shares, table_ref, out_ref, table, notes, digits, wanted, held, sem, sems):
    devices = digits.shape[0]
    each = cols // shares
    tell = pltpu.make_async_copy(table_ref.at[:, pl.ds(cols, 1)], notes, sem.at[0])
    load = pltpu.make_async_copy(table_ref.at[:, pl.ds(0, cols + 1)], table, sem.at[1])
    tell.start()
    load.start()
    tell.wait()
    for u in range(devices):
        note = notes[u, 0].astype(F32)
        digits[u : u + 1, :] = (note[:1] * DIGIT + note[1:2]).astype(jnp.int32)
    move = pltpu.make_async_copy(digits, wanted, sem.at[2])
    move.start()
    move.wait()
    load.wait()
    flat = table.reshape((devices * (cols + 1),) + table.shape[2:])
    sent = []
    for s in range(shares):

        @pl.loop(0, devices, unroll=8)
        def _(d):
            for j in range(each):
                held[s, d, j] = flat[wanted[d, s * each + j]]

        copy = pltpu.make_async_copy(held.at[s], out_ref.at[pl.ds(s * devices, devices)], sems.at[s])
        copy.start()
        sent.append(copy)
    for copy in sent:
        copy.wait()


def pick(table, cols, shares):
    devices, _, rows, width = table.shape
    each = cols // shares
    return pl.pallas_call(
        functools.partial(pick_kernel, cols, shares),
        in_specs=[HBM],
        out_specs=HBM,
        out_shape=jax.ShapeDtypeStruct((shares * devices, each, rows, width), table.dtype),
        scratch_shapes=[
            pltpu.VMEM((devices, cols + 1, rows, width), table.dtype),
            pltpu.VMEM((devices, 1, rows, width), table.dtype),
            pltpu.VMEM((devices, width), jnp.int32),
            pltpu.SMEM((devices, width), jnp.int32),
            pltpu.VMEM((shares, devices, each, rows, width), table.dtype),
            pltpu.SemaphoreType.DMA((3,)),
            pltpu.SemaphoreType.DMA((shares,)),
        ],
        compiler_params=params(56),
    )(table)


def near_kernel(info_ref, own_ref, p1_ref, p2_ref, p3_ref, blocks_ref, near_ref, turned_ref, start_ref):
    samp, rows, width = info_ref[0], own_ref.shape[0], own_ref.shape[1]
    for k, ref in enumerate((own_ref, p1_ref, p2_ref, p3_ref)):
        q = lax.rem(samp + 4 - k, 4)
        at = pl.multiple_of(q * rows, rows)
        x = ref[...]
        near_ref[0, pl.ds(at, rows), :] = x
        turned_ref[0, :, pl.ds(at, rows)] = x.T
    where_diag = info_ref[2 + pl.program_id(0)]
    start_ref[0, :width] = blocks_ref[0, where_diag]
    start_ref[0, width:] = blocks_ref[0, 1 - where_diag]


def near_panels(info, observed, received, blocks, each):
    rows, width = observed.shape[0], blocks.shape[-1]
    part = pl.BlockSpec((rows, width), lambda j, f: (0, j))
    return pl.pallas_call(
        near_kernel,
        grid_spec=pltpu.PrefetchScalarGridSpec(
            num_scalar_prefetch=1,
            grid=(each,),
            in_specs=[
                pl.BlockSpec((rows, width), lambda j, f: (0, f[1] + j)),
                part,
                part,
                part,
                pl.BlockSpec((1, 2, width, width), lambda j, f: (f[1] + j, 0, 0, 0)),
            ],
            out_specs=[
                pl.BlockSpec((1, 4 * rows, width), lambda j, f: (j, 0, 0)),
                pl.BlockSpec((1, width, 4 * rows), lambda j, f: (j, 0, 0)),
                pl.BlockSpec((1, 2 * width, width), lambda j, f: (j, 0, 0)),
            ],
        ),
        out_shape=[
            jax.ShapeDtypeStruct((each, 4 * rows, width), BF16),
            jax.ShapeDtypeStruct((each, width, 4 * rows), BF16),
            jax.ShapeDtypeStruct((each, 2 * width, width), F32),
        ],
        compiler_params=params(56),
        cost_estimate=cost(1 << 20, 10 << 20),
    )(info, observed, *received, blocks)


def shrink(v, level):
    return jnp.where(v > level, v - level, jnp.where(v < -level, v + level, 0.0))


def split3(g):
    hi = g.astype(BF16)
    rest = g - hi.astype(F32)
    mid = rest.astype(BF16)
    return hi, mid, (rest - mid.astype(F32)).astype(BF16)


def steps_kernel(first, info_ref, far_ref, near_ref, turned_ref, start_ref, diag_ref, out_ref, obj_ref):
    count, total_rows, width = far_ref.shape
    eye = lax.broadcasted_iota(jnp.int32, (width, width), 0) == lax.broadcasted_iota(jnp.int32, (width, width), 1)
    each = range(count)
    grams = []
    for c in each:
        far = far_ref[c]
        both = jnp.concatenate([near_ref[first + c], far], axis=1)
        top = jnp.dot(turned_ref[first + c], both, preferred_element_type=F32)
        low = lax.dot_general(far, both, (((0,), (0,)), ((), ())), preferred_element_type=F32)
        grams.append(split3(jnp.concatenate([top, low], axis=0)))
    db = [jnp.where(eye, 0.0, start_ref[first + c, :width]) for c in each]
    ob = [start_ref[first + c, width:] for c in each]
    dv = [diag_ref[pl.ds(info_ref[1] + first + c, 1), :] for c in each]
    lane = lax.broadcasted_iota(jnp.int32, (1, width), 1)
    total = jnp.zeros((1, width), F32)
    for i in range(STEPS):
        w = [
            jnp.concatenate([jnp.where(eye, jnp.broadcast_to(dv[c], (width, width)), db[c]), ob[c]], axis=0).astype(BF16)
            for c in each
        ]
        g = [sum(jnp.dot(p, w[c], preferred_element_type=F32) for p in reversed(grams[c])) for c in each]
        part = jnp.zeros((1, width), F32)
        for c in each:
            fit = jnp.sum(w[c].astype(F32) * g[c], axis=0, keepdims=True) / (2.0 * total_rows)
            size = jnp.sum(jnp.abs(db[c]) + jnp.abs(ob[c]), axis=0, keepdims=True)
            part = part + (fit - jnp.log(dv[c]) + PENALTY * size)
        total = jnp.where(lane == i, jnp.sum(part, axis=1, keepdims=True), total)
        for c in each:
            gd, go = g[c][:width] / total_rows, g[c][width:] / total_rows
            along = jnp.sum(jnp.where(eye, gd, 0.0), axis=0, keepdims=True)
            db[c] = jnp.where(eye, 0.0, shrink(db[c] - STEP_LENGTH * gd, STEP_LENGTH * PENALTY))
            ob[c] = shrink(ob[c] - STEP_LENGTH * go, STEP_LENGTH * PENALTY)
            m = dv[c] - STEP_LENGTH * along
            dv[c] = 0.5 * (m + jnp.sqrt(m * m + 4.0 * STEP_LENGTH))
    obj_ref[...] = total
    for c in each:
        where_diag = info_ref[2 + first + c]
        full = jnp.where(eye, jnp.broadcast_to(dv[c], (width, width)), db[c])
        out_ref[c, where_diag] = full.astype(out_ref.dtype)
        out_ref[c, 1 - where_diag] = ob[c].astype(out_ref.dtype)


def iterate(first, info, far, near, turned, start, diag_rows):
    count, width = far.shape[0], far.shape[2]
    return pl.pallas_call(
        functools.partial(steps_kernel, first),
        in_specs=[pl.BlockSpec(memory_space=pltpu.SMEM)] + [VMEM] * 5,
        out_specs=[VMEM] * 2,
        out_shape=[
            jax.ShapeDtypeStruct((count, 2, width, width), BF16),
            jax.ShapeDtypeStruct((1, width), F32),
        ],
        compiler_params=params(16),
        cost_estimate=cost(count << 29, 4 << 20),
    )(info, far, near, turned, start, diag_rows)


def put(which_ref, out_ref, diag_ref, share, half, count, at, ref):
    j = pl.program_id(0)
    column = (share * HALVES + half) * count + j
    width = ref.shape[-1]
    eye = lax.broadcasted_iota(jnp.int32, (width, width), 0) == lax.broadcasted_iota(jnp.int32, (width, width), 1)
    where_diag = which_ref[column]
    full = ref[0, where_diag].astype(F32)
    diag_ref[pl.ds(column, 1), :] = jnp.sum(jnp.where(eye, full, 0.0), axis=0, keepdims=True)
    out_ref[at, half, 0, where_diag] = jnp.where(eye, 0.0, full)
    out_ref[at, half, 0, 1 - where_diag] = ref[0, 1 - where_diag].astype(F32)


def first_places_kernel(count, samp_ref, which_ref, h00, h01, h10, h11, h30, h31, out_ref, diag_ref):
    for k, refs in ((0, (h00, h01)), (1, (h10, h11)), (3, (h30, h31))):
        q = lax.rem(samp_ref[0] + 4 - k, 4)
        for h, ref in enumerate(refs):
            put(which_ref, out_ref, diag_ref, q, h, count, q, ref)


def last_places_kernel(count, samp_ref, which_ref, h20, h21, _, old_diag_ref, out_ref, diag_ref):
    q = lax.rem(samp_ref[0] + 2, 4)

    @pl.when(pl.program_id(0) == 0)
    def _():
        diag_ref[...] = old_diag_ref[...]

    for h, ref in enumerate((h20, h21)):
        put(which_ref, out_ref, diag_ref, q, h, count, 0, ref)


def place_blocks(samp, which, own, one, three, two):
    count, tail = own[0].shape[0], own[0].shape[1:]
    zeros = (0,) * len(tail)
    part = pl.BlockSpec((1,) + tail, lambda j, f, w: (j,) + zeros)
    diag = pl.BlockSpec((4 * HALVES * count, tail[-1]), lambda j, f, w: (0, 0))
    shapes = [
        jax.ShapeDtypeStruct((4, HALVES, count) + tail, F32),
        jax.ShapeDtypeStruct((4 * HALVES * count, tail[-1]), F32),
    ]
    out, diagonal = pl.pallas_call(
        functools.partial(first_places_kernel, count),
        grid_spec=pltpu.PrefetchScalarGridSpec(
            num_scalar_prefetch=2,
            grid=(count,),
            in_specs=[part] * 6,
            out_specs=[pl.BlockSpec((4, HALVES, 1) + tail, lambda j, f, w: (0, 0, j) + zeros), diag],
        ),
        out_shape=shapes,
        compiler_params=params(24),
        cost_estimate=cost(1 << 20, 6 << 20),
    )(samp[None], which, *own, *one, *three)
    out, diagonal = pl.pallas_call(
        functools.partial(last_places_kernel, count),
        grid_spec=pltpu.PrefetchScalarGridSpec(
            num_scalar_prefetch=2,
            grid=(count,),
            in_specs=[part, part, ANY, diag],
            out_specs=[
                pl.BlockSpec((1, HALVES, 1) + tail, lambda j, f, w: (lax.rem(f[0] + 2, 4), 0, j) + zeros),
                diag,
            ],
        ),
        out_shape=shapes,
        input_output_aliases={4: 0},
        compiler_params=params(16),
        cost_estimate=cost(1 << 20, 2 << 20),
    )(samp[None], which, *two, out, diagonal)
    return out.reshape((4 * HALVES * count,) + tail), diagonal.reshape(-1)


def body(observed, blocks, diagonal, pattern):
    cols, _, width, _ = blocks.shape
    rows = observed.shape[0]
    devices = lax.axis_size(VAR)
    shares = lax.axis_size("samp")
    each = cols // shares
    half = each // HALVES
    total_rows = rows * shares
    samp = lax.axis_index("samp").astype(jnp.int32)
    var_index = lax.axis_index(VAR).astype(jnp.int32)

    pieces = cut(var_index, pattern, observed, devices, cols, width)
    panel = each * width
    received = [shift(lax.dynamic_slice_in_dim(observed, lax.rem(samp + k, shares) * panel, panel, 1), "samp", k) for k in (1, 2, 3)]
    table = lax.all_to_all(pieces, VAR, split_axis=0, concat_axis=0, tiled=True)
    start = samp * each
    columns = var_index * cols + jnp.arange(cols, dtype=jnp.int32)
    which = jnp.where(pattern[:, 0] == columns, 0, 1).astype(jnp.int32)
    info = jnp.concatenate([jnp.stack([samp, start]), lax.dynamic_slice_in_dim(which, start, each, 0)])
    near, turned, begin = near_panels(info, observed, received, blocks, each)
    outgoing = pick(table, cols, shares)
    far = lax.all_to_all(outgoing, ALL, split_axis=0, concat_axis=0, tiled=True)

    diag_rows = diagonal.reshape(cols, width)
    new, objs = [], []
    for h in range(HALVES):
        far_h = far[:, h * half : (h + 1) * half].transpose(1, 0, 2, 3).reshape(half, total_rows, width)
        done = iterate(h * half, info, far_h, near, turned, begin, diag_rows)
        new.append(done[0])
        objs.append(done[1])

    one = [shift(x, "samp", 1) for x in new]
    three = [shift(x, "samp", 3) for x in new]
    two = [shift(one[0], "samp", 1), shift(three[1], "samp", 3)]
    new_blocks, new_diagonal = place_blocks(samp, which, new, one, three, two)

    mine = jnp.broadcast_to(objs[0] + objs[1], (shares * devices, width))
    objective = jnp.sum(lax.all_to_all(mine, ALL, split_axis=0, concat_axis=0, tiled=True), axis=0)
    return (new_blocks, new_diagonal, objective[:STEPS] / (cols * devices * width))


def solution(mesh):
    torus = Mesh(mesh.devices.reshape(mesh.shape["samp"], 4, 8, 2), ALL)
    placed = (P("samp", VAR), P(VAR, None, None, None), P(VAR), P(VAR, None))
    return jax.shard_map(
        body,
        mesh=torus,
        in_specs=placed,
        out_specs=(P(VAR, None, None, None), P(VAR), P()),
        check_vma=False,
    )
```

```python
import functools

import jax
import jax.numpy as jnp
from jax import lax
from jax.experimental import pallas as pl
from jax.experimental.pallas import tpu as pltpu
from jax.sharding import Mesh
from jax.sharding import PartitionSpec as P

STEPS = 2
STEP_LENGTH = 0.5
PENALTY = 0.5
DIGIT = 64
HALVES = 2
VAR = ("var_0", "var_1", "var_2")
ALL = ("samp", "var_0", "var_1", "var_2")
F32 = jnp.float32
BF16 = jnp.bfloat16
VMEM = pl.BlockSpec(memory_space=pltpu.VMEM)
ANY = pl.BlockSpec(memory_space=pl.ANY)
HBM = pl.BlockSpec(memory_space=pltpu.HBM)


def params(mib):
    return pltpu.CompilerParams(vmem_limit_bytes=mib << 20)


def cost(flops, bytes_accessed):
    return pl.CostEstimate(flops=flops, bytes_accessed=bytes_accessed, transcendentals=0)


def shift(x, axis, k):
    n = lax.axis_size(axis)
    return lax.ppermute(x, axis, [(i, (i + k) % n) for i in range(n)])


def cut_kernel(cols, at_ref, pattern_ref, data_ref, out_ref):
    tiles, _, halves, rows, width = data_ref.shape
    for t in range(tiles):
        for b in range(cols):
            for h in range(halves):
                out_ref[t, h, b] = data_ref[t, b, h]
    first, second = pattern_ref[0:1, :], pattern_ref[1:2, :]
    lane = lax.broadcasted_iota(jnp.int32, first.shape, 1)
    block = jnp.where(first == at_ref[0] * cols + lane, second, first)
    place = block + lax.div(block, cols)
    digits = jnp.concatenate([lax.div(place, DIGIT), lax.rem(place, DIGIT)], axis=0).astype(F32)
    wide = jnp.concatenate([digits, jnp.zeros((rows - 2, cols), F32)], axis=0)
    wide = jnp.concatenate([wide, jnp.zeros((rows, width - cols), F32)], axis=1).astype(out_ref.dtype)
    for t in range(tiles):
        for h in range(halves):
            out_ref[t, h, cols] = wide


def cut(var_index, pattern, data, devices, cols, width):
    rows = data.shape[0] // devices
    tiles = devices // 2
    view = data.reshape(tiles, 2 * rows, cols, width).transpose(0, 2, 1, 3).reshape(tiles, cols, 2, rows, width)
    block = 4
    out = pl.pallas_call(
        functools.partial(cut_kernel, cols),
        grid=(tiles // block,),
        in_specs=[
            pl.BlockSpec(memory_space=pltpu.SMEM),
            pl.BlockSpec((2, cols), lambda i: (0, 0)),
            pl.BlockSpec((block, cols, 2, rows, width), lambda i: (i, 0, 0, 0, 0)),
        ],
        out_specs=pl.BlockSpec((block, 2, cols + 1, rows, width), lambda i: (i, 0, 0, 0, 0)),
        out_shape=jax.ShapeDtypeStruct((tiles, 2, cols + 1, rows, width), data.dtype),
        compiler_params=params(56),
    )(var_index[None], pattern.T, view)
    return out.reshape(devices, cols + 1, rows, width)


def pick_kernel(cols, shares, table_ref, *rest):
    out_ref, table, notes, digits, wanted, held, sem, sems = rest[-8:]
    devices = digits.shape[0]
    each = cols // shares
    tell = pltpu.make_async_copy(table_ref.at[:, pl.ds(cols, 1)], notes, sem.at[0])
    load = pltpu.make_async_copy(table_ref.at[:, pl.ds(0, cols + 1)], table, sem.at[1])
    tell.start()
    load.start()
    tell.wait()
    for u in range(devices):
        note = notes[u, 0].astype(F32)
        digits[u : u + 1, :] = (note[:1] * DIGIT + note[1:2]).astype(jnp.int32)
    move = pltpu.make_async_copy(digits, wanted, sem.at[2])
    move.start()
    move.wait()
    load.wait()
    flat = table.reshape((devices * (cols + 1),) + table.shape[2:])
    sent = []
    for s in range(shares):

        @pl.loop(0, devices, unroll=8)
        def _(d):
            for j in range(each):
                held[s, d, j] = flat[wanted[d, s * each + j]]

        copy = pltpu.make_async_copy(held.at[s], out_ref.at[pl.ds(s * devices, devices)], sems.at[s])
        copy.start()
        sent.append(copy)
    for copy in sent:
        copy.wait()


def pick(table, cols, shares, after):
    devices, _, rows, width = table.shape
    each = cols // shares
    return pl.pallas_call(
        functools.partial(pick_kernel, cols, shares),
        in_specs=[HBM] + [HBM] * len(after),
        out_specs=HBM,
        out_shape=jax.ShapeDtypeStruct((shares * devices, each, rows, width), table.dtype),
        scratch_shapes=[
            pltpu.VMEM((devices, cols + 1, rows, width), table.dtype),
            pltpu.VMEM((devices, 1, rows, width), table.dtype),
            pltpu.VMEM((devices, width), jnp.int32),
            pltpu.SMEM((devices, width), jnp.int32),
            pltpu.VMEM((shares, devices, each, rows, width), table.dtype),
            pltpu.SemaphoreType.DMA((3,)),
            pltpu.SemaphoreType.DMA((shares,)),
        ],
        compiler_params=params(56),
    )(table, *after)


def near_kernel(info_ref, own_ref, p1_ref, p2_ref, p3_ref, blocks_ref, near_ref, turned_ref, start_ref):
    samp, rows, width = info_ref[0], own_ref.shape[0], own_ref.shape[1]
    for k, ref in enumerate((own_ref, p1_ref, p2_ref, p3_ref)):
        q = lax.rem(samp + 4 - k, 4)
        at = pl.multiple_of(q * rows, rows)
        x = ref[...]
        near_ref[0, pl.ds(at, rows), :] = x
        turned_ref[0, :, pl.ds(at, rows)] = x.T
    where_diag = info_ref[2 + pl.program_id(0)]
    start_ref[0, :width] = blocks_ref[0, where_diag]
    start_ref[0, width:] = blocks_ref[0, 1 - where_diag]


def near_panels(info, observed, received, blocks, each):
    rows, width = observed.shape[0], blocks.shape[-1]
    part = pl.BlockSpec((rows, width), lambda j, f: (0, j))
    return pl.pallas_call(
        near_kernel,
        grid_spec=pltpu.PrefetchScalarGridSpec(
            num_scalar_prefetch=1,
            grid=(each,),
            in_specs=[
                pl.BlockSpec((rows, width), lambda j, f: (0, f[1] + j)),
                part,
                part,
                part,
                pl.BlockSpec((1, 2, width, width), lambda j, f: (f[1] + j, 0, 0, 0)),
            ],
            out_specs=[
                pl.BlockSpec((1, 4 * rows, width), lambda j, f: (j, 0, 0)),
                pl.BlockSpec((1, width, 4 * rows), lambda j, f: (j, 0, 0)),
                pl.BlockSpec((1, 2 * width, width), lambda j, f: (j, 0, 0)),
            ],
        ),
        out_shape=[
            jax.ShapeDtypeStruct((each, 4 * rows, width), BF16),
            jax.ShapeDtypeStruct((each, width, 4 * rows), BF16),
            jax.ShapeDtypeStruct((each, 2 * width, width), F32),
        ],
        compiler_params=params(56),
        cost_estimate=cost(1 << 20, 10 << 20),
    )(info, observed, *received, blocks)


def shrink(v, level):
    return jnp.where(v > level, v - level, jnp.where(v < -level, v + level, 0.0))


def split3(g):
    hi = g.astype(BF16)
    rest = g - hi.astype(F32)
    mid = rest.astype(BF16)
    return hi, mid, (rest - mid.astype(F32)).astype(BF16)


def steps_kernel(first, info_ref, far_ref, near_ref, turned_ref, start_ref, diag_ref, out_ref, obj_ref):
    count, total_rows, width = far_ref.shape
    eye = lax.broadcasted_iota(jnp.int32, (width, width), 0) == lax.broadcasted_iota(jnp.int32, (width, width), 1)
    each = range(count)
    grams = []
    for c in each:
        far = far_ref[c]
        both = jnp.concatenate([near_ref[first + c], far], axis=1)
        top = jnp.dot(turned_ref[first + c], both, preferred_element_type=F32)
        low = lax.dot_general(far, both, (((0,), (0,)), ((), ())), preferred_element_type=F32)
        grams.append(split3(jnp.concatenate([top, low], axis=0)))
    db = [jnp.where(eye, 0.0, start_ref[first + c, :width]) for c in each]
    ob = [start_ref[first + c, width:] for c in each]
    dv = [diag_ref[pl.ds(info_ref[1] + first + c, 1), :] for c in each]
    lane = lax.broadcasted_iota(jnp.int32, (1, width), 1)
    total = jnp.zeros((1, width), F32)
    for i in range(STEPS):
        w = [
            jnp.concatenate([jnp.where(eye, jnp.broadcast_to(dv[c], (width, width)), db[c]), ob[c]], axis=0).astype(BF16)
            for c in each
        ]
        g = [sum(jnp.dot(p, w[c], preferred_element_type=F32) for p in reversed(grams[c])) for c in each]
        part = jnp.zeros((1, width), F32)
        for c in each:
            fit = jnp.sum(w[c].astype(F32) * g[c], axis=0, keepdims=True) / (2.0 * total_rows)
            size = jnp.sum(jnp.abs(db[c]) + jnp.abs(ob[c]), axis=0, keepdims=True)
            part = part + (fit - jnp.log(dv[c]) + PENALTY * size)
        total = jnp.where(lane == i, jnp.sum(part, axis=1, keepdims=True), total)
        for c in each:
            gd, go = g[c][:width] / total_rows, g[c][width:] / total_rows
            along = jnp.sum(jnp.where(eye, gd, 0.0), axis=0, keepdims=True)
            db[c] = jnp.where(eye, 0.0, shrink(db[c] - STEP_LENGTH * gd, STEP_LENGTH * PENALTY))
            ob[c] = shrink(ob[c] - STEP_LENGTH * go, STEP_LENGTH * PENALTY)
            m = dv[c] - STEP_LENGTH * along
            dv[c] = 0.5 * (m + jnp.sqrt(m * m + 4.0 * STEP_LENGTH))
    obj_ref[...] = total
    for c in each:
        where_diag = info_ref[2 + first + c]
        full = jnp.where(eye, jnp.broadcast_to(dv[c], (width, width)), db[c])
        out_ref[c, where_diag] = full.astype(out_ref.dtype)
        out_ref[c, 1 - where_diag] = ob[c].astype(out_ref.dtype)


def iterate(first, info, far, near, turned, start, diag_rows):
    count, width = far.shape[0], far.shape[2]
    return pl.pallas_call(
        functools.partial(steps_kernel, first),
        in_specs=[pl.BlockSpec(memory_space=pltpu.SMEM)] + [VMEM] * 5,
        out_specs=[VMEM] * 2,
        out_shape=[
            jax.ShapeDtypeStruct((count, 2, width, width), BF16),
            jax.ShapeDtypeStruct((1, width), F32),
        ],
        compiler_params=params(16),
        cost_estimate=cost(count << 29, 4 << 20),
    )(info, far, near, turned, start, diag_rows)


def put(which_ref, out_ref, diag_ref, share, half, count, at, ref):
    j = pl.program_id(0)
    column = (share * HALVES + half) * count + j
    width = ref.shape[-1]
    eye = lax.broadcasted_iota(jnp.int32, (width, width), 0) == lax.broadcasted_iota(jnp.int32, (width, width), 1)
    where_diag = which_ref[column]
    full = ref[0, where_diag].astype(F32)
    diag_ref[pl.ds(column, 1), :] = jnp.sum(jnp.where(eye, full, 0.0), axis=0, keepdims=True)
    out_ref[at, half, 0, where_diag] = jnp.where(eye, 0.0, full)
    out_ref[at, half, 0, 1 - where_diag] = ref[0, 1 - where_diag].astype(F32)


def first_places_kernel(count, samp_ref, which_ref, h00, h01, h10, h11, h30, h31, out_ref, diag_ref):
    for k, refs in ((0, (h00, h01)), (1, (h10, h11)), (3, (h30, h31))):
        q = lax.rem(samp_ref[0] + 4 - k, 4)
        for h, ref in enumerate(refs):
            put(which_ref, out_ref, diag_ref, q, h, count, q, ref)


def last_places_kernel(count, samp_ref, which_ref, h20, h21, _, old_diag_ref, out_ref, diag_ref):
    q = lax.rem(samp_ref[0] + 2, 4)

    @pl.when(pl.program_id(0) == 0)
    def _():
        diag_ref[...] = old_diag_ref[...]

    for h, ref in enumerate((h20, h21)):
        put(which_ref, out_ref, diag_ref, q, h, count, 0, ref)


def place_blocks(samp, which, own, one, three, two):
    count, tail = own[0].shape[0], own[0].shape[1:]
    zeros = (0,) * len(tail)
    part = pl.BlockSpec((1,) + tail, lambda j, f, w: (j,) + zeros)
    diag = pl.BlockSpec((4 * HALVES * count, tail[-1]), lambda j, f, w: (0, 0))
    shapes = [
        jax.ShapeDtypeStruct((4, HALVES, count) + tail, F32),
        jax.ShapeDtypeStruct((4 * HALVES * count, tail[-1]), F32),
    ]
    out, diagonal = pl.pallas_call(
        functools.partial(first_places_kernel, count),
        grid_spec=pltpu.PrefetchScalarGridSpec(
            num_scalar_prefetch=2,
            grid=(count,),
            in_specs=[part] * 6,
            out_specs=[pl.BlockSpec((4, HALVES, 1) + tail, lambda j, f, w: (0, 0, j) + zeros), diag],
        ),
        out_shape=shapes,
        compiler_params=params(24),
        cost_estimate=cost(1 << 20, 6 << 20),
    )(samp[None], which, *own, *one, *three)
    out, diagonal = pl.pallas_call(
        functools.partial(last_places_kernel, count),
        grid_spec=pltpu.PrefetchScalarGridSpec(
            num_scalar_prefetch=2,
            grid=(count,),
            in_specs=[part, part, ANY, diag],
            out_specs=[
                pl.BlockSpec((1, HALVES, 1) + tail, lambda j, f, w: (lax.rem(f[0] + 2, 4), 0, j) + zeros),
                diag,
            ],
        ),
        out_shape=shapes,
        input_output_aliases={4: 0},
        compiler_params=params(16),
        cost_estimate=cost(1 << 20, 2 << 20),
    )(samp[None], which, *two, out, diagonal)
    return out.reshape((4 * HALVES * count,) + tail), diagonal.reshape(-1)


def body(observed, blocks, diagonal, pattern):
    cols, _, width, _ = blocks.shape
    rows = observed.shape[0]
    devices = lax.axis_size(VAR)
    shares = lax.axis_size("samp")
    each = cols // shares
    half = each // HALVES
    total_rows = rows * shares
    samp = lax.axis_index("samp").astype(jnp.int32)
    var_index = lax.axis_index(VAR).astype(jnp.int32)

    pieces = cut(var_index, pattern, observed, devices, cols, width)
    panel = each * width
    received = [shift(lax.dynamic_slice_in_dim(observed, lax.rem(samp + k, shares) * panel, panel, 1), "samp", k) for k in (1, 2, 3)]
    table = lax.all_to_all(pieces, VAR, split_axis=0, concat_axis=0, tiled=True)
    start = samp * each
    columns = var_index * cols + jnp.arange(cols, dtype=jnp.int32)
    which = jnp.where(pattern[:, 0] == columns, 0, 1).astype(jnp.int32)
    info = jnp.concatenate([jnp.stack([samp, start]), lax.dynamic_slice_in_dim(which, start, each, 0)])
    near, turned, begin = near_panels(info, observed, received, blocks, each)
    outgoing = pick(table, cols, shares, (near, turned, begin))
    far = lax.all_to_all(outgoing, ALL, split_axis=0, concat_axis=0, tiled=True)

    diag_rows = diagonal.reshape(cols, width)
    new, objs = [], []
    for h in range(HALVES):
        far_h = far[:, h * half : (h + 1) * half].transpose(1, 0, 2, 3).reshape(half, total_rows, width)
        done = iterate(h * half, info, far_h, near, turned, begin, diag_rows)
        new.append(done[0])
        objs.append(done[1])

    one = [shift(x, "samp", 1) for x in new]
    three = [shift(x, "samp", 3) for x in new]
    two = [shift(one[0], "samp", 1), shift(three[1], "samp", 3)]
    new_blocks, new_diagonal = place_blocks(samp, which, new, one, three, two)

    later = jnp.minimum(jnp.abs(three[1][0, 0, 0].astype(F32)), 0.0)
    mine = jnp.broadcast_to(objs[0] + objs[1] + later, (shares * devices, width))
    objective = jnp.sum(lax.all_to_all(mine, ALL, split_axis=0, concat_axis=0, tiled=True), axis=0)
    return (new_blocks, new_diagonal, objective[:STEPS] / (cols * devices * width))


def solution(mesh):
    torus = Mesh(mesh.devices.reshape(mesh.shape["samp"], 4, 8, 2), ALL)
    placed = (P("samp", VAR), P(VAR, None, None, None), P(VAR), P(VAR, None))
    return jax.shard_map(
        body,
        mesh=torus,
        in_specs=placed,
        out_specs=(P(VAR, None, None, None), P(VAR), P()),
        check_vma=False,
    )
```

```python
import functools

import jax
import jax.numpy as jnp
from jax import lax
from jax.experimental import pallas as pl
from jax.experimental.pallas import tpu as pltpu
from jax.sharding import Mesh
from jax.sharding import PartitionSpec as P

STEPS = 2
STEP_LENGTH = 0.5
PENALTY = 0.5
DIGIT = 64
VAR = ("var_0", "var_1", "var_2")
ALL = ("samp", "var_0", "var_1", "var_2")
F32 = jnp.float32
BF16 = jnp.bfloat16
VMEM = pl.BlockSpec(memory_space=pltpu.VMEM)
ANY = pl.BlockSpec(memory_space=pl.ANY)
HBM = pl.BlockSpec(memory_space=pltpu.HBM)


def params(mib):
    return pltpu.CompilerParams(vmem_limit_bytes=mib << 20)


def cost(flops, bytes_accessed):
    return pl.CostEstimate(flops=flops, bytes_accessed=bytes_accessed, transcendentals=0)


def shift(x, axis, k):
    n = lax.axis_size(axis)
    return lax.ppermute(x, axis, [(i, (i + k) % n) for i in range(n)])


def cut_kernel(cols, chunks, at_ref, pattern_ref, data_ref, out_ref, held, cutting, in_sems, out_sems):
    tiles, _, halves, rows, width = data_ref.shape
    each = tiles // chunks
    loads = [
        pltpu.make_async_copy(data_ref.at[pl.ds(i * each, each)], held.at[pl.ds(i * each, each)], in_sems.at[i])
        for i in range(chunks)
    ]
    for load in loads:
        load.start()
    first, second = pattern_ref[0:1, :], pattern_ref[1:2, :]
    lane = lax.broadcasted_iota(jnp.int32, first.shape, 1)
    block = jnp.where(first == at_ref[0] * cols + lane, second, first)
    place = block + lax.div(block, cols)
    digits = jnp.concatenate([lax.div(place, DIGIT), lax.rem(place, DIGIT)], axis=0).astype(F32)
    wide = jnp.concatenate([digits, jnp.zeros((rows - 2, cols), F32)], axis=0)
    wide = jnp.concatenate([wide, jnp.zeros((rows, width - cols), F32)], axis=1).astype(out_ref.dtype)
    for t in range(tiles):
        for h in range(halves):
            cutting[t, h, cols] = wide
    stores = []
    for i, load in enumerate(loads):
        load.wait()

        @pl.loop(i * each, (i + 1) * each)
        def _(t):
            for b in range(cols):
                for h in range(halves):
                    cutting[t, h, b] = held[t, b, h]

        store = pltpu.make_async_copy(cutting.at[pl.ds(i * each, each)], out_ref.at[pl.ds(i * each, each)], out_sems.at[i])
        store.start()
        stores.append(store)
    for store in stores:
        store.wait()


def cut(var_index, pattern, data, devices, cols, width):
    rows = data.shape[0] // devices
    tiles = devices // 2
    view = data.reshape(tiles, 2 * rows, cols, width).transpose(0, 2, 1, 3).reshape(tiles, cols, 2, rows, width)
    chunks = 4
    shape = (tiles, 2, cols + 1, rows, width)
    out = pl.pallas_call(
        functools.partial(cut_kernel, cols, chunks),
        in_specs=[pl.BlockSpec(memory_space=pltpu.SMEM), VMEM, HBM],
        out_specs=HBM,
        out_shape=jax.ShapeDtypeStruct(shape, data.dtype),
        scratch_shapes=[
            pltpu.VMEM(view.shape, data.dtype),
            pltpu.VMEM(shape, data.dtype),
            pltpu.SemaphoreType.DMA((chunks,)),
            pltpu.SemaphoreType.DMA((chunks,)),
        ],
        compiler_params=params(56),
    )(var_index[None], pattern.T, view)
    return out.reshape(devices, cols + 1, rows, width)


def pick_kernel(cols, shares, table_ref, *rest):
    out_ref, table, notes, digits, wanted, held, sem, sems = rest[-8:]
    devices = digits.shape[0]
    each = cols // shares
    tell = pltpu.make_async_copy(table_ref.at[:, pl.ds(cols, 1)], notes, sem.at[0])
    load = pltpu.make_async_copy(table_ref.at[:, pl.ds(0, cols + 1)], table, sem.at[1])
    tell.start()
    load.start()
    tell.wait()
    for u in range(devices):
        note = notes[u, 0].astype(F32)
        digits[u : u + 1, :] = (note[:1] * DIGIT + note[1:2]).astype(jnp.int32)
    move = pltpu.make_async_copy(digits, wanted, sem.at[2])
    move.start()
    move.wait()
    load.wait()
    flat = table.reshape((devices * (cols + 1),) + table.shape[2:])
    sent = []
    for s in range(shares):

        @pl.loop(0, devices, unroll=8)
        def _(d):
            for j in range(each):
                held[s, d, j] = flat[wanted[d, s * each + j]]

        copy = pltpu.make_async_copy(held.at[s], out_ref.at[pl.ds(s * devices, devices)], sems.at[s])
        copy.start()
        sent.append(copy)
    for copy in sent:
        copy.wait()


def pick(table, cols, shares, after):
    devices, _, rows, width = table.shape
    each = cols // shares
    return pl.pallas_call(
        functools.partial(pick_kernel, cols, shares),
        in_specs=[HBM] + [HBM] * len(after),
        out_specs=HBM,
        out_shape=jax.ShapeDtypeStruct((shares * devices, each, rows, width), table.dtype),
        scratch_shapes=[
            pltpu.VMEM((devices, cols + 1, rows, width), table.dtype),
            pltpu.VMEM((devices, 1, rows, width), table.dtype),
            pltpu.VMEM((devices, width), jnp.int32),
            pltpu.SMEM((devices, width), jnp.int32),
            pltpu.VMEM((shares, devices, each, rows, width), table.dtype),
            pltpu.SemaphoreType.DMA((3,)),
            pltpu.SemaphoreType.DMA((shares,)),
        ],
        compiler_params=params(56),
    )(table, *after)


def near_kernel(info_ref, own_ref, p1_ref, p2_ref, p3_ref, blocks_ref, near_ref, turned_ref, start_ref):
    samp, rows, width = info_ref[0], own_ref.shape[0], own_ref.shape[1]
    for k, ref in enumerate((own_ref, p1_ref, p2_ref, p3_ref)):
        q = lax.rem(samp + 4 - k, 4)
        at = pl.multiple_of(q * rows, rows)
        x = ref[...]
        near_ref[0, pl.ds(at, rows), :] = x
        turned_ref[0, :, pl.ds(at, rows)] = x.T
    where_diag = info_ref[2 + pl.program_id(0)]
    start_ref[0, :width] = blocks_ref[0, where_diag]
    start_ref[0, width:] = blocks_ref[0, 1 - where_diag]


def near_panels(info, observed, received, blocks, each):
    rows, width = observed.shape[0], blocks.shape[-1]
    part = pl.BlockSpec((rows, width), lambda j, f: (0, j))
    return pl.pallas_call(
        near_kernel,
        grid_spec=pltpu.PrefetchScalarGridSpec(
            num_scalar_prefetch=1,
            grid=(each,),
            in_specs=[
                pl.BlockSpec((rows, width), lambda j, f: (0, f[1] + j)),
                part,
                part,
                part,
                pl.BlockSpec((1, 2, width, width), lambda j, f: (f[1] + j, 0, 0, 0)),
            ],
            out_specs=[
                pl.BlockSpec((1, 4 * rows, width), lambda j, f: (j, 0, 0)),
                pl.BlockSpec((1, width, 4 * rows), lambda j, f: (j, 0, 0)),
                pl.BlockSpec((1, 2 * width, width), lambda j, f: (j, 0, 0)),
            ],
        ),
        out_shape=[
            jax.ShapeDtypeStruct((each, 4 * rows, width), BF16),
            jax.ShapeDtypeStruct((each, width, 4 * rows), BF16),
            jax.ShapeDtypeStruct((each, 2 * width, width), F32),
        ],
        compiler_params=params(56),
        cost_estimate=cost(1 << 20, 10 << 20),
    )(info, observed, *received, blocks)


def shrink(v, level):
    return jnp.where(v > level, v - level, jnp.where(v < -level, v + level, 0.0))


def split3(g):
    hi = g.astype(BF16)
    rest = g - hi.astype(F32)
    mid = rest.astype(BF16)
    return hi, mid, (rest - mid.astype(F32)).astype(BF16)


def steps_kernel(info_ref, far_ref, near_ref, turned_ref, start_ref, diag_ref, out_ref, obj_ref):
    count, total_rows, width = far_ref.shape
    eye = lax.broadcasted_iota(jnp.int32, (width, width), 0) == lax.broadcasted_iota(jnp.int32, (width, width), 1)
    each = range(count)
    grams = []
    for c in each:
        far = far_ref[c]
        both = jnp.concatenate([near_ref[c], far], axis=1)
        top = jnp.dot(turned_ref[c], both, preferred_element_type=F32)
        low = lax.dot_general(far, both, (((0,), (0,)), ((), ())), preferred_element_type=F32)
        grams.append(split3(jnp.concatenate([top, low], axis=0)))
    db = [jnp.where(eye, 0.0, start_ref[c, :width]) for c in each]
    ob = [start_ref[c, width:] for c in each]
    dv = [diag_ref[pl.ds(info_ref[1] + c, 1), :] for c in each]
    lane = lax.broadcasted_iota(jnp.int32, (1, width), 1)
    total = jnp.zeros((1, width), F32)
    for i in range(STEPS):
        w = [
            jnp.concatenate([jnp.where(eye, jnp.broadcast_to(dv[c], (width, width)), db[c]), ob[c]], axis=0).astype(BF16)
            for c in each
        ]
        g = [sum(jnp.dot(p, w[c], preferred_element_type=F32) for p in reversed(grams[c])) for c in each]
        part = jnp.zeros((1, width), F32)
        for c in each:
            fit = jnp.sum(w[c].astype(F32) * g[c], axis=0, keepdims=True) / (2.0 * total_rows)
            size = jnp.sum(jnp.abs(db[c]) + jnp.abs(ob[c]), axis=0, keepdims=True)
            part = part + (fit - jnp.log(dv[c]) + PENALTY * size)
        total = jnp.where(lane == i, jnp.sum(part, axis=1, keepdims=True), total)
        for c in each:
            gd, go = g[c][:width] / total_rows, g[c][width:] / total_rows
            along = jnp.sum(jnp.where(eye, gd, 0.0), axis=0, keepdims=True)
            db[c] = jnp.where(eye, 0.0, shrink(db[c] - STEP_LENGTH * gd, STEP_LENGTH * PENALTY))
            ob[c] = shrink(ob[c] - STEP_LENGTH * go, STEP_LENGTH * PENALTY)
            m = dv[c] - STEP_LENGTH * along
            dv[c] = 0.5 * (m + jnp.sqrt(m * m + 4.0 * STEP_LENGTH))
    obj_ref[...] = total
    for c in each:
        where_diag = info_ref[2 + c]
        full = jnp.where(eye, jnp.broadcast_to(dv[c], (width, width)), db[c])
        out_ref[c, where_diag] = full.astype(out_ref.dtype)
        out_ref[c, 1 - where_diag] = ob[c].astype(out_ref.dtype)


def iterate(info, far, near, turned, start, diag_rows):
    count, width = far.shape[0], far.shape[2]
    return pl.pallas_call(
        steps_kernel,
        in_specs=[pl.BlockSpec(memory_space=pltpu.SMEM)] + [VMEM] * 5,
        out_specs=[VMEM] * 2,
        out_shape=[
            jax.ShapeDtypeStruct((count, 2, width, width), BF16),
            jax.ShapeDtypeStruct((1, width), F32),
        ],
        compiler_params=params(24),
        cost_estimate=cost(count << 29, 4 << 20),
    )(info, far, near, turned, start, diag_rows)


def put(which_ref, out_ref, diag_ref, at, column, ref):
    width = ref.shape[-1]
    eye = lax.broadcasted_iota(jnp.int32, (width, width), 0) == lax.broadcasted_iota(jnp.int32, (width, width), 1)
    where_diag = which_ref[column]
    full = ref[0, where_diag].astype(F32)
    diag_ref[pl.ds(column, 1), :] = jnp.sum(jnp.where(eye, full, 0.0), axis=0, keepdims=True)
    out_ref[at, 0, where_diag] = jnp.where(eye, 0.0, full)
    out_ref[at, 0, 1 - where_diag] = ref[0, 1 - where_diag].astype(F32)


def first_places_kernel(samp_ref, which_ref, own_ref, one_ref, three_ref, out_ref, diag_ref):
    for k, ref in ((0, own_ref), (1, one_ref), (3, three_ref)):
        q = lax.rem(samp_ref[0] + 4 - k, 4)
        put(which_ref, out_ref, diag_ref, q, q * pl.num_programs(0) + pl.program_id(0), ref)


def last_places_kernel(samp_ref, which_ref, low_ref, high_ref, _, old_diag_ref, out_ref, diag_ref):
    j, half = pl.program_id(0), pl.num_programs(0)
    column = lax.rem(samp_ref[0] + 2, 4) * 2 * half + j

    @pl.when(j == 0)
    def _():
        diag_ref[...] = old_diag_ref[...]

    for h, ref in enumerate((low_ref, high_ref)):
        put(which_ref, out_ref.at[0], diag_ref, h, column + h * half, ref)


def place_blocks(samp, which, own, one, three, two):
    count, tail = own.shape[0], own.shape[1:]
    half = count // 2
    zeros = (0,) * len(tail)
    part = pl.BlockSpec((1,) + tail, lambda j, f, w: (j,) + zeros)
    diag = pl.BlockSpec((4 * count, tail[-1]), lambda j, f, w: (0, 0))
    shape = (4, count) + tail
    diag_shape = jax.ShapeDtypeStruct((4 * count, tail[-1]), F32)
    out, diagonal = pl.pallas_call(
        first_places_kernel,
        grid_spec=pltpu.PrefetchScalarGridSpec(
            num_scalar_prefetch=2,
            grid=(count,),
            in_specs=[part] * 3,
            out_specs=[pl.BlockSpec((4, 1) + tail, lambda j, f, w: (0, j) + zeros), diag],
        ),
        out_shape=[jax.ShapeDtypeStruct(shape, F32), diag_shape],
        compiler_params=params(24),
        cost_estimate=cost(1 << 20, 6 << 20),
    )(samp[None], which, own, one, three)
    shape = (4, 2, half) + tail
    out, diagonal = pl.pallas_call(
        last_places_kernel,
        grid_spec=pltpu.PrefetchScalarGridSpec(
            num_scalar_prefetch=2,
            grid=(half,),
            in_specs=[part, part, ANY, diag],
            out_specs=[
                pl.BlockSpec((1, 2, 1) + tail, lambda j, f, w: (lax.rem(f[0] + 2, 4), 0, j) + zeros),
                diag,
            ],
        ),
        out_shape=[jax.ShapeDtypeStruct(shape, F32), diag_shape],
        input_output_aliases={4: 0},
        compiler_params=params(16),
        cost_estimate=cost(1 << 20, 2 << 20),
    )(samp[None], which, *two, out.reshape(shape), diagonal)
    return out.reshape((4 * count,) + tail), diagonal.reshape(-1)


def body(observed, blocks, diagonal, pattern):
    cols, _, width, _ = blocks.shape
    rows = observed.shape[0]
    devices = lax.axis_size(VAR)
    shares = lax.axis_size("samp")
    each = cols // shares
    total_rows = rows * shares
    samp = lax.axis_index("samp").astype(jnp.int32)
    var_index = lax.axis_index(VAR).astype(jnp.int32)

    pieces = cut(var_index, pattern, observed, devices, cols, width)
    panel = each * width
    received = [shift(lax.dynamic_slice_in_dim(observed, lax.rem(samp + k, shares) * panel, panel, 1), "samp", k) for k in (1, 2, 3)]
    table = lax.all_to_all(pieces, VAR, split_axis=0, concat_axis=0, tiled=True)
    start = samp * each
    columns = var_index * cols + jnp.arange(cols, dtype=jnp.int32)
    which = jnp.where(pattern[:, 0] == columns, 0, 1).astype(jnp.int32)
    info = jnp.concatenate([jnp.stack([samp, start]), lax.dynamic_slice_in_dim(which, start, each, 0)])
    near, turned, begin = near_panels(info, observed, received, blocks, each)
    outgoing = pick(table, cols, shares, (near, turned, begin))
    far = lax.all_to_all(outgoing, ALL, split_axis=0, concat_axis=0, tiled=True)

    diag_rows = diagonal.reshape(cols, width)
    far = far.transpose(1, 0, 2, 3).reshape(each, total_rows, width)
    new, obj = iterate(info, far, near, turned, begin, diag_rows)
    one, three = shift(new, "samp", 1), shift(new, "samp", 3)
    two = [shift(one[: each // 2], "samp", 1), shift(three[each // 2 :], "samp", 3)]
    new_blocks, new_diagonal = place_blocks(samp, which, new, one, three, two)

    obj = jnp.broadcast_to(obj, (devices, width))
    obj = jnp.sum(lax.all_to_all(obj, VAR, split_axis=0, concat_axis=0, tiled=True), axis=0, keepdims=True)
    objective = ((obj + shift(obj, "samp", 2)) + (shift(obj, "samp", 1) + shift(obj, "samp", 3)))[0]
    return (new_blocks, new_diagonal, objective[:STEPS] / (cols * devices * width))


def solution(mesh):
    torus = Mesh(mesh.devices.reshape(mesh.shape["samp"], 4, 8, 2), ALL)
    placed = (P("samp", VAR), P(VAR, None, None, None), P(VAR), P(VAR, None))
    return jax.shard_map(
        body,
        mesh=torus,
        in_specs=placed,
        out_specs=(P(VAR, None, None, None), P(VAR), P()),
        check_vma=False,
    )
```

```python
import functools

import jax
import jax.numpy as jnp
from jax import lax
from jax.experimental import pallas as pl
from jax.experimental.pallas import tpu as pltpu
from jax.sharding import Mesh
from jax.sharding import PartitionSpec as P

STEPS = 2
STEP_LENGTH = 0.5
PENALTY = 0.5
DIGIT = 64
VAR = ("var_0", "var_1", "var_2")
ALL = ("samp", "var_0", "var_1", "var_2")
F32 = jnp.float32
BF16 = jnp.bfloat16
VMEM = pl.BlockSpec(memory_space=pltpu.VMEM)
ANY = pl.BlockSpec(memory_space=pl.ANY)
HBM = pl.BlockSpec(memory_space=pltpu.HBM)


def params(mib):
    return pltpu.CompilerParams(vmem_limit_bytes=mib << 20)


def cost(flops, bytes_accessed):
    return pl.CostEstimate(flops=flops, bytes_accessed=bytes_accessed, transcendentals=0)


def shift(x, axis, k):
    n = lax.axis_size(axis)
    return lax.ppermute(x, axis, [(i, (i + k) % n) for i in range(n)])


def cut_kernel(cols, chunks, at_ref, pattern_ref, data_ref, out_ref, held, cutting, in_sems, out_sems):
    tiles, _, halves, rows, width = data_ref.shape
    each = tiles // chunks
    loads = [
        pltpu.make_async_copy(data_ref.at[pl.ds(i * each, each)], held.at[pl.ds(i * each, each)], in_sems.at[i])
        for i in range(chunks)
    ]
    for load in loads:
        load.start()
    first, second = pattern_ref[0:1, :], pattern_ref[1:2, :]
    lane = lax.broadcasted_iota(jnp.int32, first.shape, 1)
    block = jnp.where(first == at_ref[0] * cols + lane, second, first)
    place = block + lax.div(block, cols)
    digits = jnp.concatenate([lax.div(place, DIGIT), lax.rem(place, DIGIT)], axis=0).astype(F32)
    wide = jnp.concatenate([digits, jnp.zeros((rows - 2, cols), F32)], axis=0)
    wide = jnp.concatenate([wide, jnp.zeros((rows, width - cols), F32)], axis=1).astype(out_ref.dtype)
    for t in range(tiles):
        for h in range(halves):
            cutting[t, h, cols] = wide
    stores = []
    for i, load in enumerate(loads):
        load.wait()

        @pl.loop(i * each, (i + 1) * each)
        def _(t):
            for b in range(cols):
                for h in range(halves):
                    cutting[t, h, b] = held[t, b, h]

        store = pltpu.make_async_copy(cutting.at[pl.ds(i * each, each)], out_ref.at[pl.ds(i * each, each)], out_sems.at[i])
        store.start()
        stores.append(store)
    for store in stores:
        store.wait()


def cut(var_index, pattern, data, devices, cols, width):
    rows = data.shape[0] // devices
    tiles = devices // 2
    view = data.reshape(tiles, 2 * rows, cols, width).transpose(0, 2, 1, 3).reshape(tiles, cols, 2, rows, width)
    chunks = 4
    shape = (tiles, 2, cols + 1, rows, width)
    out = pl.pallas_call(
        functools.partial(cut_kernel, cols, chunks),
        in_specs=[pl.BlockSpec(memory_space=pltpu.SMEM), VMEM, HBM],
        out_specs=HBM,
        out_shape=jax.ShapeDtypeStruct(shape, data.dtype),
        scratch_shapes=[
            pltpu.VMEM(view.shape, data.dtype),
            pltpu.VMEM(shape, data.dtype),
            pltpu.SemaphoreType.DMA((chunks,)),
            pltpu.SemaphoreType.DMA((chunks,)),
        ],
        compiler_params=params(56),
    )(var_index[None], pattern.T, view)
    return out.reshape(devices, cols + 1, rows, width)


def pick_kernel(cols, shares, table_ref, *rest):
    out_ref, table, notes, digits, wanted, held, sem, sems = rest[-8:]
    devices = digits.shape[0]
    each = cols // shares
    tell = pltpu.make_async_copy(table_ref.at[:, pl.ds(cols, 1)], notes, sem.at[0])
    load = pltpu.make_async_copy(table_ref.at[:, pl.ds(0, cols + 1)], table, sem.at[1])
    tell.start()
    load.start()
    tell.wait()
    for u in range(devices):
        note = notes[u, 0].astype(F32)
        digits[u : u + 1, :] = (note[:1] * DIGIT + note[1:2]).astype(jnp.int32)
    move = pltpu.make_async_copy(digits, wanted, sem.at[2])
    move.start()
    move.wait()
    load.wait()
    flat = table.reshape((devices * (cols + 1),) + table.shape[2:])
    sent = []
    for s in range(shares):

        @pl.loop(0, devices, unroll=8)
        def _(d):
            for j in range(each):
                held[s, d, j] = flat[wanted[d, s * each + j]]

        copy = pltpu.make_async_copy(held.at[s], out_ref.at[pl.ds(s * devices, devices)], sems.at[s])
        copy.start()
        sent.append(copy)
    for copy in sent:
        copy.wait()


def pick(table, cols, shares, after):
    devices, _, rows, width = table.shape
    each = cols // shares
    return pl.pallas_call(
        functools.partial(pick_kernel, cols, shares),
        in_specs=[HBM] + [HBM] * len(after),
        out_specs=HBM,
        out_shape=jax.ShapeDtypeStruct((shares * devices, each, rows, width), table.dtype),
        scratch_shapes=[
            pltpu.VMEM((devices, cols + 1, rows, width), table.dtype),
            pltpu.VMEM((devices, 1, rows, width), table.dtype),
            pltpu.VMEM((devices, width), jnp.int32),
            pltpu.SMEM((devices, width), jnp.int32),
            pltpu.VMEM((shares, devices, each, rows, width), table.dtype),
            pltpu.SemaphoreType.DMA((3,)),
            pltpu.SemaphoreType.DMA((shares,)),
        ],
        compiler_params=params(56),
    )(table, *after)


def near_kernel(info_ref, own_ref, p1_ref, p2_ref, p3_ref, blocks_ref, near_ref, turned_ref, start_ref):
    samp, rows, width = info_ref[0], own_ref.shape[0], own_ref.shape[1]
    for k, ref in enumerate((own_ref, p1_ref, p2_ref, p3_ref)):
        q = lax.rem(samp + 4 - k, 4)
        at = pl.multiple_of(q * rows, rows)
        x = ref[...]
        near_ref[0, pl.ds(at, rows), :] = x
        turned_ref[0, :, pl.ds(at, rows)] = x.T
    where_diag = info_ref[2 + pl.program_id(0)]
    start_ref[0, :width] = blocks_ref[0, where_diag]
    start_ref[0, width:] = blocks_ref[0, 1 - where_diag]


def near_panels(info, observed, received, blocks, each):
    rows, width = observed.shape[0], blocks.shape[-1]
    part = pl.BlockSpec((rows, width), lambda j, f: (0, j))
    return pl.pallas_call(
        near_kernel,
        grid_spec=pltpu.PrefetchScalarGridSpec(
            num_scalar_prefetch=1,
            grid=(each,),
            in_specs=[
                pl.BlockSpec((rows, width), lambda j, f: (0, f[1] + j)),
                part,
                part,
                part,
                pl.BlockSpec((1, 2, width, width), lambda j, f: (f[1] + j, 0, 0, 0)),
            ],
            out_specs=[
                pl.BlockSpec((1, 4 * rows, width), lambda j, f: (j, 0, 0)),
                pl.BlockSpec((1, width, 4 * rows), lambda j, f: (j, 0, 0)),
                pl.BlockSpec((1, 2 * width, width), lambda j, f: (j, 0, 0)),
            ],
        ),
        out_shape=[
            jax.ShapeDtypeStruct((each, 4 * rows, width), BF16),
            jax.ShapeDtypeStruct((each, width, 4 * rows), BF16),
            jax.ShapeDtypeStruct((each, 2 * width, width), F32),
        ],
        compiler_params=params(56),
        cost_estimate=cost(1 << 20, 10 << 20),
    )(info, observed, *received, blocks)


def shrink(v, level):
    return jnp.where(v > level, v - level, jnp.where(v < -level, v + level, 0.0))


def split3(g):
    hi = g.astype(BF16)
    rest = g - hi.astype(F32)
    mid = rest.astype(BF16)
    return hi, mid, (rest - mid.astype(F32)).astype(BF16)


def steps_kernel(info_ref, far_ref, near_ref, turned_ref, start_ref, diag_ref, out_ref, obj_ref):
    count, total_rows, width = far_ref.shape
    eye = lax.broadcasted_iota(jnp.int32, (width, width), 0) == lax.broadcasted_iota(jnp.int32, (width, width), 1)
    each = range(count)
    grams = []
    for c in each:
        far = far_ref[c]
        both = jnp.concatenate([near_ref[c], far], axis=1)
        top = jnp.dot(turned_ref[c], both, preferred_element_type=F32)
        low = lax.dot_general(far, both, (((0,), (0,)), ((), ())), preferred_element_type=F32)
        grams.append(split3(jnp.concatenate([top, low], axis=0)))
    db = [jnp.where(eye, 0.0, start_ref[c, :width]) for c in each]
    ob = [start_ref[c, width:] for c in each]
    dv = [diag_ref[pl.ds(info_ref[1] + c, 1), :] for c in each]
    lane = lax.broadcasted_iota(jnp.int32, (1, width), 1)
    total = jnp.zeros((1, width), F32)
    for i in range(STEPS):
        w = [
            jnp.concatenate([jnp.where(eye, jnp.broadcast_to(dv[c], (width, width)), db[c]), ob[c]], axis=0).astype(BF16)
            for c in each
        ]
        g = [sum(jnp.dot(p, w[c], preferred_element_type=F32) for p in reversed(grams[c])) for c in each]
        part = jnp.zeros((1, width), F32)
        for c in each:
            fit = jnp.sum(w[c].astype(F32) * g[c], axis=0, keepdims=True) / (2.0 * total_rows)
            size = jnp.sum(jnp.abs(db[c]) + jnp.abs(ob[c]), axis=0, keepdims=True)
            part = part + (fit - jnp.log(dv[c]) + PENALTY * size)
        total = jnp.where(lane == i, jnp.sum(part, axis=1, keepdims=True), total)
        for c in each:
            gd, go = g[c][:width] / total_rows, g[c][width:] / total_rows
            along = jnp.sum(jnp.where(eye, gd, 0.0), axis=0, keepdims=True)
            db[c] = jnp.where(eye, 0.0, shrink(db[c] - STEP_LENGTH * gd, STEP_LENGTH * PENALTY))
            ob[c] = shrink(ob[c] - STEP_LENGTH * go, STEP_LENGTH * PENALTY)
            m = dv[c] - STEP_LENGTH * along
            dv[c] = 0.5 * (m + jnp.sqrt(m * m + 4.0 * STEP_LENGTH))
    obj_ref[...] = total
    for c in each:
        where_diag = info_ref[2 + c]
        full = jnp.where(eye, jnp.broadcast_to(dv[c], (width, width)), db[c])
        out_ref[c, where_diag] = full.astype(out_ref.dtype)
        out_ref[c, 1 - where_diag] = ob[c].astype(out_ref.dtype)


def iterate(info, far, near, turned, start, diag_rows):
    count, width = far.shape[0], far.shape[2]
    return pl.pallas_call(
        steps_kernel,
        in_specs=[pl.BlockSpec(memory_space=pltpu.SMEM)] + [VMEM] * 5,
        out_specs=[VMEM] * 2,
        out_shape=[
            jax.ShapeDtypeStruct((count, 2, width, width), BF16),
            jax.ShapeDtypeStruct((1, width), F32),
        ],
        compiler_params=params(24),
        cost_estimate=cost(count << 29, 4 << 20),
    )(info, far, near, turned, start, diag_rows)


def put(which_ref, out_ref, diag_ref, at, column, block):
    width = block.shape[-1]
    eye = lax.broadcasted_iota(jnp.int32, (width, width), 0) == lax.broadcasted_iota(jnp.int32, (width, width), 1)
    where_diag = which_ref[column]
    full = block[where_diag].astype(F32)
    diag_ref[pl.ds(column, 1), :] = jnp.sum(jnp.where(eye, full, 0.0), axis=0, keepdims=True)
    out_ref[at + (where_diag,)] = jnp.where(eye, 0.0, full)
    out_ref[at + (1 - where_diag,)] = block[1 - where_diag].astype(F32)


def first_places_kernel(samp_ref, which_ref, own_ref, one_ref, three_ref, out_ref, diag_ref):
    @pl.when(pl.program_id(0) == 0)
    def _():
        diag_ref[...] = jnp.zeros_like(diag_ref)

    block = own_ref.shape[0]
    for k, ref in ((0, own_ref), (1, one_ref), (3, three_ref)):
        q = lax.rem(samp_ref[0] + 4 - k, 4)
        for c in range(block):
            put(which_ref, out_ref, diag_ref, (q, c), (q * pl.num_programs(0) + pl.program_id(0)) * block + c, ref.at[c])


def last_places_kernel(samp_ref, which_ref, low_ref, high_ref, _, old_diag_ref, out_ref, diag_ref):
    @pl.when(pl.program_id(0) == 0)
    def _():
        diag_ref[...] = old_diag_ref[...]

    block = low_ref.shape[0]
    half = pl.num_programs(0) * block
    for h, ref in enumerate((low_ref, high_ref)):
        for c in range(block):
            column = (lax.rem(samp_ref[0] + 2, 4) * 2 + h) * half + pl.program_id(0) * block + c
            put(which_ref, out_ref, diag_ref, (0, h, c), column, ref.at[c])


def place_first(samp, which, own, one, three):
    count, tail = own.shape[0], own.shape[1:]
    zeros = (0,) * len(tail)
    block = 2
    part = pl.BlockSpec((block,) + tail, lambda j, f, w: (j,) + zeros)
    return pl.pallas_call(
        first_places_kernel,
        grid_spec=pltpu.PrefetchScalarGridSpec(
            num_scalar_prefetch=2,
            grid=(count // block,),
            in_specs=[part] * 3,
            out_specs=[
                pl.BlockSpec((4, block) + tail, lambda j, f, w: (0, j) + zeros),
                pl.BlockSpec((4 * count, tail[-1]), lambda j, f, w: (0, 0)),
            ],
        ),
        out_shape=[jax.ShapeDtypeStruct((4, count) + tail, F32), jax.ShapeDtypeStruct((4 * count, tail[-1]), F32)],
        compiler_params=params(24),
        cost_estimate=cost(1 << 20, 6 << 20),
    )(samp[None], which, own, one, three)


def place_last(samp, which, low, high, out, diagonal):
    half, tail = low.shape[0], low.shape[1:]
    zeros = (0,) * len(tail)
    block = 2
    shape = (4, 2, half) + tail
    part = pl.BlockSpec((block,) + tail, lambda j, f, w: (j,) + zeros)
    diag = pl.BlockSpec(diagonal.shape, lambda j, f, w: (0, 0))
    out, diagonal = pl.pallas_call(
        last_places_kernel,
        grid_spec=pltpu.PrefetchScalarGridSpec(
            num_scalar_prefetch=2,
            grid=(half // block,),
            in_specs=[part, part, ANY, diag],
            out_specs=[
                pl.BlockSpec((1, 2, block) + tail, lambda j, f, w: (lax.rem(f[0] + 2, 4), 0, j) + zeros),
                diag,
            ],
        ),
        out_shape=[
            jax.ShapeDtypeStruct(shape, F32),
            jax.ShapeDtypeStruct(diagonal.shape, F32),
        ],
        input_output_aliases={4: 0},
        compiler_params=params(16),
        cost_estimate=cost(1 << 20, 2 << 20),
    )(samp[None], which, low, high, out.reshape(shape), diagonal)
    return out.reshape((8 * half,) + tail), diagonal.reshape(-1)


def body(observed, blocks, diagonal, pattern):
    cols, _, width, _ = blocks.shape
    rows = observed.shape[0]
    devices = lax.axis_size(VAR)
    shares = lax.axis_size("samp")
    each = cols // shares
    total_rows = rows * shares
    samp = lax.axis_index("samp").astype(jnp.int32)
    var_index = lax.axis_index(VAR).astype(jnp.int32)

    pieces = cut(var_index, pattern, observed, devices, cols, width)
    panel = each * width
    received = [shift(lax.dynamic_slice_in_dim(observed, lax.rem(samp + k, shares) * panel, panel, 1), "samp", k) for k in (1, 2, 3)]
    table = lax.all_to_all(pieces, VAR, split_axis=0, concat_axis=0, tiled=True)
    start = samp * each
    columns = var_index * cols + jnp.arange(cols, dtype=jnp.int32)
    which = jnp.where(pattern[:, 0] == columns, 0, 1).astype(jnp.int32)
    info = jnp.concatenate([jnp.stack([samp, start]), lax.dynamic_slice_in_dim(which, start, each, 0)])
    near, turned, begin = near_panels(info, observed, received, blocks, each)
    outgoing = pick(table, cols, shares, (near, turned, begin))
    far = lax.all_to_all(outgoing, ALL, split_axis=0, concat_axis=0, tiled=True)

    diag_rows = diagonal.reshape(cols, width)
    far = far.transpose(1, 0, 2, 3).reshape(each, total_rows, width)
    new, obj = iterate(info, far, near, turned, begin, diag_rows)
    one, three = shift(new, "samp", 1), shift(new, "samp", 3)
    two = [shift(one[: each // 2], "samp", 1), shift(three[each // 2 :], "samp", 3)]
    terms = jnp.broadcast_to(obj[None], (shares * devices, 1, width))
    terms = jnp.sum(lax.all_to_all(terms, ALL, split_axis=0, concat_axis=0, tiled=True), axis=(0, 1))
    placed, diag = place_first(samp, which, new, one, three)
    new_blocks, new_diagonal = place_last(samp, which, *two, placed, diag)
    return (new_blocks, new_diagonal, terms[:STEPS] / (cols * devices * width))


def solution(mesh):
    torus = Mesh(mesh.devices.reshape(mesh.shape["samp"], 4, 8, 2), ALL)
    placed = (P("samp", VAR), P(VAR, None, None, None), P(VAR), P(VAR, None))
    return jax.shard_map(
        body,
        mesh=torus,
        in_specs=placed,
        out_specs=(P(VAR, None, None, None), P(VAR), P()),
        check_vma=False,
    )
```

```python
import functools

import jax
import jax.numpy as jnp
from jax import lax
from jax.experimental import pallas as pl
from jax.experimental.pallas import tpu as pltpu
from jax.sharding import Mesh
from jax.sharding import PartitionSpec as P

STEPS = 2
STEP_LENGTH = 0.5
PENALTY = 0.5
DIGIT = 64
VAR = ("var_0", "var_1", "var_2")
ALL = ("samp", "var_0", "var_1", "var_2")
F32 = jnp.float32
BF16 = jnp.bfloat16
VMEM = pl.BlockSpec(memory_space=pltpu.VMEM)
ANY = pl.BlockSpec(memory_space=pl.ANY)
HBM = pl.BlockSpec(memory_space=pltpu.HBM)


def params(mib):
    return pltpu.CompilerParams(vmem_limit_bytes=mib << 20)


def cost(flops, bytes_accessed):
    return pl.CostEstimate(flops=flops, bytes_accessed=bytes_accessed, transcendentals=0)


def shift(x, axis, k):
    n = lax.axis_size(axis)
    return lax.ppermute(x, axis, [(i, (i + k) % n) for i in range(n)])


def cut_kernel(cols, chunks, at_ref, pattern_ref, data_ref, out_ref, held, cutting, in_sems, out_sems):
    tiles, _, halves, rows, width = data_ref.shape
    each = tiles // chunks
    loads = [
        pltpu.make_async_copy(data_ref.at[pl.ds(i * each, each)], held.at[pl.ds(i * each, each)], in_sems.at[i])
        for i in range(chunks)
    ]
    for load in loads:
        load.start()
    first, second = pattern_ref[0:1, :], pattern_ref[1:2, :]
    lane = lax.broadcasted_iota(jnp.int32, first.shape, 1)
    block = jnp.where(first == at_ref[0] * cols + lane, second, first)
    place = block + lax.div(block, cols)
    digits = jnp.concatenate([lax.div(place, DIGIT), lax.rem(place, DIGIT)], axis=0).astype(F32)
    wide = jnp.concatenate([digits, jnp.zeros((rows - 2, cols), F32)], axis=0)
    wide = jnp.concatenate([wide, jnp.zeros((rows, width - cols), F32)], axis=1).astype(out_ref.dtype)
    for t in range(tiles):
        for h in range(halves):
            cutting[t, h, cols] = wide
    stores = []
    for i, load in enumerate(loads):
        load.wait()

        @pl.loop(i * each, (i + 1) * each)
        def _(t):
            for b in range(cols):
                for h in range(halves):
                    cutting[t, h, b] = held[t, b, h]

        store = pltpu.make_async_copy(cutting.at[pl.ds(i * each, each)], out_ref.at[pl.ds(i * each, each)], out_sems.at[i])
        store.start()
        stores.append(store)
    for store in stores:
        store.wait()


def cut(var_index, pattern, data, devices, cols, width):
    rows = data.shape[0] // devices
    tiles = devices // 2
    view = data.reshape(tiles, 2 * rows, cols, width).transpose(0, 2, 1, 3).reshape(tiles, cols, 2, rows, width)
    chunks = 4
    shape = (tiles, 2, cols + 1, rows, width)
    out = pl.pallas_call(
        functools.partial(cut_kernel, cols, chunks),
        in_specs=[pl.BlockSpec(memory_space=pltpu.SMEM), VMEM, HBM],
        out_specs=HBM,
        out_shape=jax.ShapeDtypeStruct(shape, data.dtype),
        scratch_shapes=[
            pltpu.VMEM(view.shape, data.dtype),
            pltpu.VMEM(shape, data.dtype),
            pltpu.SemaphoreType.DMA((chunks,)),
            pltpu.SemaphoreType.DMA((chunks,)),
        ],
        compiler_params=params(56),
    )(var_index[None], pattern.T, view)
    return out.reshape(devices, cols + 1, rows, width)


def pick_kernel(cols, shares, table_ref, *rest):
    out_ref, table, notes, digits, wanted, held, sem, sems = rest[-8:]
    devices = digits.shape[0]
    each = cols // shares
    tell = pltpu.make_async_copy(table_ref.at[:, pl.ds(cols, 1)], notes, sem.at[0])
    load = pltpu.make_async_copy(table_ref.at[:, pl.ds(0, cols + 1)], table, sem.at[1])
    tell.start()
    load.start()
    tell.wait()
    for u in range(devices):
        note = notes[u, 0].astype(F32)
        digits[u : u + 1, :] = (note[:1] * DIGIT + note[1:2]).astype(jnp.int32)
    move = pltpu.make_async_copy(digits, wanted, sem.at[2])
    move.start()
    move.wait()
    load.wait()
    flat = table.reshape((devices * (cols + 1),) + table.shape[2:])
    sent = []
    for s in range(shares):

        @pl.loop(0, devices, unroll=8)
        def _(d):
            for j in range(each):
                held[s, d, j] = flat[wanted[d, s * each + j]]

        copy = pltpu.make_async_copy(held.at[s], out_ref.at[pl.ds(s * devices, devices)], sems.at[s])
        copy.start()
        sent.append(copy)
    for copy in sent:
        copy.wait()


def pick(table, cols, shares, after):
    devices, _, rows, width = table.shape
    each = cols // shares
    return pl.pallas_call(
        functools.partial(pick_kernel, cols, shares),
        in_specs=[HBM] + [HBM] * len(after),
        out_specs=HBM,
        out_shape=jax.ShapeDtypeStruct((shares * devices, each, rows, width), table.dtype),
        scratch_shapes=[
            pltpu.VMEM((devices, cols + 1, rows, width), table.dtype),
            pltpu.VMEM((devices, 1, rows, width), table.dtype),
            pltpu.VMEM((devices, width), jnp.int32),
            pltpu.SMEM((devices, width), jnp.int32),
            pltpu.VMEM((shares, devices, each, rows, width), table.dtype),
            pltpu.SemaphoreType.DMA((3,)),
            pltpu.SemaphoreType.DMA((shares,)),
        ],
        compiler_params=params(56),
    )(table, *after)


def near_kernel(info_ref, own_ref, p1_ref, p2_ref, p3_ref, blocks_ref, near_ref, turned_ref, start_ref):
    samp, rows, width = info_ref[0], own_ref.shape[0], own_ref.shape[1]
    for k, ref in enumerate((own_ref, p1_ref, p2_ref, p3_ref)):
        q = lax.rem(samp + 4 - k, 4)
        at = pl.multiple_of(q * rows, rows)
        x = ref[...]
        near_ref[0, pl.ds(at, rows), :] = x
        turned_ref[0, :, pl.ds(at, rows)] = x.T
    where_diag = info_ref[2 + pl.program_id(0)]
    start_ref[0, :width] = blocks_ref[0, where_diag]
    start_ref[0, width:] = blocks_ref[0, 1 - where_diag]


def near_panels(info, observed, received, blocks, each):
    rows, width = observed.shape[0], blocks.shape[-1]
    part = pl.BlockSpec((rows, width), lambda j, f: (0, j))
    return pl.pallas_call(
        near_kernel,
        grid_spec=pltpu.PrefetchScalarGridSpec(
            num_scalar_prefetch=1,
            grid=(each,),
            in_specs=[
                pl.BlockSpec((rows, width), lambda j, f: (0, f[1] + j)),
                part,
                part,
                part,
                pl.BlockSpec((1, 2, width, width), lambda j, f: (f[1] + j, 0, 0, 0)),
            ],
            out_specs=[
                pl.BlockSpec((1, 4 * rows, width), lambda j, f: (j, 0, 0)),
                pl.BlockSpec((1, width, 4 * rows), lambda j, f: (j, 0, 0)),
                pl.BlockSpec((1, 2 * width, width), lambda j, f: (j, 0, 0)),
            ],
        ),
        out_shape=[
            jax.ShapeDtypeStruct((each, 4 * rows, width), BF16),
            jax.ShapeDtypeStruct((each, width, 4 * rows), BF16),
            jax.ShapeDtypeStruct((each, 2 * width, width), F32),
        ],
        compiler_params=params(56),
        cost_estimate=cost(1 << 20, 10 << 20),
    )(info, observed, *received, blocks)


def shrink(v, level):
    return jnp.where(v > level, v - level, jnp.where(v < -level, v + level, 0.0))


def split3(g):
    hi = g.astype(BF16)
    rest = g - hi.astype(F32)
    mid = rest.astype(BF16)
    return hi, mid, (rest - mid.astype(F32)).astype(BF16)


def steps_kernel(info_ref, far_ref, near_ref, turned_ref, start_ref, diag_ref, out_ref, obj_ref):
    count, total_rows, width = far_ref.shape
    eye = lax.broadcasted_iota(jnp.int32, (width, width), 0) == lax.broadcasted_iota(jnp.int32, (width, width), 1)
    each = range(count)
    grams = []
    for c in each:
        far = far_ref[c]
        both = jnp.concatenate([near_ref[c], far], axis=1)
        top = jnp.dot(turned_ref[c], both, preferred_element_type=F32)
        low = lax.dot_general(far, both, (((0,), (0,)), ((), ())), preferred_element_type=F32)
        grams.append(split3(jnp.concatenate([top, low], axis=0)))
    db = [jnp.where(eye, 0.0, start_ref[c, :width]) for c in each]
    ob = [start_ref[c, width:] for c in each]
    dv = [diag_ref[pl.ds(info_ref[1] + c, 1), :] for c in each]
    lane = lax.broadcasted_iota(jnp.int32, (1, width), 1)
    total = jnp.zeros((1, width), F32)
    for i in range(STEPS):
        w = [
            jnp.concatenate([jnp.where(eye, jnp.broadcast_to(dv[c], (width, width)), db[c]), ob[c]], axis=0).astype(BF16)
            for c in each
        ]
        g = [sum(jnp.dot(p, w[c], preferred_element_type=F32) for p in reversed(grams[c])) for c in each]
        part = jnp.zeros((1, width), F32)
        for c in each:
            fit = jnp.sum(w[c].astype(F32) * g[c], axis=0, keepdims=True) / (2.0 * total_rows)
            size = jnp.sum(jnp.abs(db[c]) + jnp.abs(ob[c]), axis=0, keepdims=True)
            part = part + (fit - jnp.log(dv[c]) + PENALTY * size)
        total = jnp.where(lane == i, jnp.sum(part, axis=1, keepdims=True), total)
        for c in each:
            gd, go = g[c][:width] / total_rows, g[c][width:] / total_rows
            along = jnp.sum(jnp.where(eye, gd, 0.0), axis=0, keepdims=True)
            db[c] = jnp.where(eye, 0.0, shrink(db[c] - STEP_LENGTH * gd, STEP_LENGTH * PENALTY))
            ob[c] = shrink(ob[c] - STEP_LENGTH * go, STEP_LENGTH * PENALTY)
            m = dv[c] - STEP_LENGTH * along
            dv[c] = 0.5 * (m + jnp.sqrt(m * m + 4.0 * STEP_LENGTH))
    obj_ref[...] = total
    for c in each:
        where_diag = info_ref[2 + c]
        full = jnp.where(eye, jnp.broadcast_to(dv[c], (width, width)), db[c])
        out_ref[c, where_diag] = full.astype(out_ref.dtype)
        out_ref[c, 1 - where_diag] = ob[c].astype(out_ref.dtype)


def iterate(info, far, near, turned, start, diag_rows):
    count, width = far.shape[0], far.shape[2]
    return pl.pallas_call(
        steps_kernel,
        in_specs=[pl.BlockSpec(memory_space=pltpu.SMEM)] + [VMEM] * 5,
        out_specs=[VMEM] * 2,
        out_shape=[
            jax.ShapeDtypeStruct((count, 2, width, width), BF16),
            jax.ShapeDtypeStruct((1, width), F32),
        ],
        compiler_params=params(24),
        cost_estimate=cost(count << 29, 4 << 20),
    )(info, far, near, turned, start, diag_rows)


def put(which_ref, out_ref, diag_ref, at, column, block):
    width = block.shape[-1]
    eye = lax.broadcasted_iota(jnp.int32, (width, width), 0) == lax.broadcasted_iota(jnp.int32, (width, width), 1)
    where_diag = which_ref[column]
    full = block[where_diag].astype(F32)
    diag_ref[pl.ds(column, 1), :] = jnp.sum(jnp.where(eye, full, 0.0), axis=0, keepdims=True)
    out_ref[at + (where_diag,)] = jnp.where(eye, 0.0, full)
    out_ref[at + (1 - where_diag,)] = block[1 - where_diag].astype(F32)


def first_places_kernel(samp_ref, which_ref, own_ref, one_ref, three_ref, out_ref, diag_ref):
    @pl.when(pl.program_id(0) == 0)
    def _():
        diag_ref[...] = jnp.zeros_like(diag_ref)

    block = own_ref.shape[0]
    for k, ref in ((0, own_ref), (1, one_ref), (3, three_ref)):
        q = lax.rem(samp_ref[0] + 4 - k, 4)
        for c in range(block):
            put(which_ref, out_ref, diag_ref, (q, c), (q * pl.num_programs(0) + pl.program_id(0)) * block + c, ref.at[c])


def last_places_kernel(samp_ref, which_ref, low_ref, high_ref, _, old_diag_ref, out_ref, diag_ref):
    @pl.when(pl.program_id(0) == 0)
    def _():
        diag_ref[...] = old_diag_ref[...]

    block = low_ref.shape[0]
    half = pl.num_programs(0) * block
    for h, ref in enumerate((low_ref, high_ref)):
        for c in range(block):
            column = (lax.rem(samp_ref[0] + 2, 4) * 2 + h) * half + pl.program_id(0) * block + c
            put(which_ref, out_ref, diag_ref, (0, h, c), column, ref.at[c])


def place_first(samp, which, own, one, three):
    count, tail = own.shape[0], own.shape[1:]
    zeros = (0,) * len(tail)
    block = 2
    part = pl.BlockSpec((block,) + tail, lambda j, f, w: (j,) + zeros)
    return pl.pallas_call(
        first_places_kernel,
        grid_spec=pltpu.PrefetchScalarGridSpec(
            num_scalar_prefetch=2,
            grid=(count // block,),
            in_specs=[part] * 3,
            out_specs=[
                pl.BlockSpec((4, block) + tail, lambda j, f, w: (0, j) + zeros),
                pl.BlockSpec((4 * count, tail[-1]), lambda j, f, w: (0, 0)),
            ],
        ),
        out_shape=[jax.ShapeDtypeStruct((4, count) + tail, F32), jax.ShapeDtypeStruct((4 * count, tail[-1]), F32)],
        compiler_params=params(24),
        cost_estimate=cost(1 << 20, 6 << 20),
    )(samp[None], which, own, one, three)


def place_last(samp, which, low, high, out, diagonal):
    half, tail = low.shape[0], low.shape[1:]
    zeros = (0,) * len(tail)
    block = 2
    shape = (4, 2, half) + tail
    part = pl.BlockSpec((block,) + tail, lambda j, f, w: (j,) + zeros)
    diag = pl.BlockSpec(diagonal.shape, lambda j, f, w: (0, 0))
    out, diagonal = pl.pallas_call(
        last_places_kernel,
        grid_spec=pltpu.PrefetchScalarGridSpec(
            num_scalar_prefetch=2,
            grid=(half // block,),
            in_specs=[part, part, ANY, diag],
            out_specs=[
                pl.BlockSpec((1, 2, block) + tail, lambda j, f, w: (lax.rem(f[0] + 2, 4), 0, j) + zeros),
                diag,
            ],
        ),
        out_shape=[
            jax.ShapeDtypeStruct(shape, F32),
            jax.ShapeDtypeStruct(diagonal.shape, F32),
        ],
        input_output_aliases={4: 0},
        compiler_params=params(16),
        cost_estimate=cost(1 << 20, 2 << 20),
    )(samp[None], which, low, high, out.reshape(shape), diagonal)
    return out.reshape((8 * half,) + tail), diagonal.reshape(-1)


def body(observed, blocks, diagonal, pattern):
    cols, _, width, _ = blocks.shape
    rows = observed.shape[0]
    devices = lax.axis_size(VAR)
    shares = lax.axis_size("samp")
    each = cols // shares
    total_rows = rows * shares
    samp = lax.axis_index("samp").astype(jnp.int32)
    var_index = lax.axis_index(VAR).astype(jnp.int32)

    pieces = cut(var_index, pattern, observed, devices, cols, width)
    panel = each * width
    received = [shift(lax.dynamic_slice_in_dim(observed, lax.rem(samp + k, shares) * panel, panel, 1), "samp", k) for k in (1, 2, 3)]
    table = lax.all_to_all(pieces, VAR, split_axis=0, concat_axis=0, tiled=True)
    start = samp * each
    columns = var_index * cols + jnp.arange(cols, dtype=jnp.int32)
    which = jnp.where(pattern[:, 0] == columns, 0, 1).astype(jnp.int32)
    info = jnp.concatenate([jnp.stack([samp, start]), lax.dynamic_slice_in_dim(which, start, each, 0)])
    near, turned, begin = near_panels(info, observed, received, blocks, each)
    outgoing = pick(table, cols, shares, (near, turned, begin))
    far = lax.all_to_all(outgoing, ALL, split_axis=0, concat_axis=0, tiled=True)

    diag_rows = diagonal.reshape(cols, width)
    far = far.transpose(1, 0, 2, 3).reshape(each, total_rows, width)
    new, obj = iterate(info, far, near, turned, begin, diag_rows)
    one, three = shift(new, "samp", 1), shift(new, "samp", 3)
    two = [shift(one[: each // 2], "samp", 1), shift(three[each // 2 :], "samp", 3)]
    terms = jnp.broadcast_to(obj[None], (shares * devices, 1, width))
    terms = lax.all_to_all(terms, ALL, split_axis=0, concat_axis=0, tiled=True)
    placed, diag = place_first(samp, which, new, one, three)
    terms, diag = lax.optimization_barrier((terms, diag))
    terms = jnp.sum(terms, axis=(0, 1))
    new_blocks, new_diagonal = place_last(samp, which, *two, placed, diag)
    return (new_blocks, new_diagonal, terms[:STEPS] / (cols * devices * width))


def solution(mesh):
    torus = Mesh(mesh.devices.reshape(mesh.shape["samp"], 4, 8, 2), ALL)
    placed = (P("samp", VAR), P(VAR, None, None, None), P(VAR), P(VAR, None))
    return jax.shard_map(
        body,
        mesh=torus,
        in_specs=placed,
        out_specs=(P(VAR, None, None, None), P(VAR), P()),
        check_vma=False,
    )
```

```python
import functools

import jax
import jax.numpy as jnp
from jax import lax
from jax.experimental import pallas as pl
from jax.experimental.pallas import tpu as pltpu
from jax.sharding import Mesh
from jax.sharding import PartitionSpec as P

STEPS = 2
STEP_LENGTH = 0.5
PENALTY = 0.5
DIGIT = 64
VAR = ("var_0", "var_1", "var_2")
ALL = ("samp", "var_0", "var_1", "var_2")
F32 = jnp.float32
BF16 = jnp.bfloat16
VMEM = pl.BlockSpec(memory_space=pltpu.VMEM)
ANY = pl.BlockSpec(memory_space=pl.ANY)
HBM = pl.BlockSpec(memory_space=pltpu.HBM)


def params(mib):
    return pltpu.CompilerParams(vmem_limit_bytes=mib << 20)


def cost(flops, bytes_accessed):
    return pl.CostEstimate(flops=flops, bytes_accessed=bytes_accessed, transcendentals=0)


def shift(x, axis, k):
    n = lax.axis_size(axis)
    return lax.ppermute(x, axis, [(i, (i + k) % n) for i in range(n)])


def cut_kernel(cols, chunks, at_ref, pattern_ref, data_ref, out_ref, held, cutting, in_sems, out_sems):
    tiles, _, halves, rows, width = data_ref.shape
    each = tiles // chunks
    loads = [
        pltpu.make_async_copy(data_ref.at[pl.ds(i * each, each)], held.at[pl.ds(i * each, each)], in_sems.at[i])
        for i in range(chunks)
    ]
    for load in loads:
        load.start()
    first, second = pattern_ref[0:1, :], pattern_ref[1:2, :]
    lane = lax.broadcasted_iota(jnp.int32, first.shape, 1)
    block = jnp.where(first == at_ref[0] * cols + lane, second, first)
    place = block + lax.div(block, cols)
    digits = jnp.concatenate([lax.div(place, DIGIT), lax.rem(place, DIGIT)], axis=0).astype(F32)
    wide = jnp.concatenate([digits, jnp.zeros((rows - 2, cols), F32)], axis=0)
    wide = jnp.concatenate([wide, jnp.zeros((rows, width - cols), F32)], axis=1).astype(out_ref.dtype)
    for t in range(tiles):
        for h in range(halves):
            cutting[t, h, cols] = wide
    stores = []
    for i, load in enumerate(loads):
        load.wait()

        @pl.loop(i * each, (i + 1) * each)
        def _(t):
            for b in range(cols):
                for h in range(halves):
                    cutting[t, h, b] = held[t, b, h]

        store = pltpu.make_async_copy(cutting.at[pl.ds(i * each, each)], out_ref.at[pl.ds(i * each, each)], out_sems.at[i])
        store.start()
        stores.append(store)
    for store in stores:
        store.wait()


def cut(var_index, pattern, data, devices, cols, width):
    rows = data.shape[0] // devices
    tiles = devices // 2
    view = data.reshape(tiles, 2 * rows, cols, width).transpose(0, 2, 1, 3).reshape(tiles, cols, 2, rows, width)
    chunks = 8
    shape = (tiles, 2, cols + 1, rows, width)
    out = pl.pallas_call(
        functools.partial(cut_kernel, cols, chunks),
        in_specs=[pl.BlockSpec(memory_space=pltpu.SMEM), VMEM, HBM],
        out_specs=HBM,
        out_shape=jax.ShapeDtypeStruct(shape, data.dtype),
        scratch_shapes=[
            pltpu.VMEM(view.shape, data.dtype),
            pltpu.VMEM(shape, data.dtype),
            pltpu.SemaphoreType.DMA((chunks,)),
            pltpu.SemaphoreType.DMA((chunks,)),
        ],
        compiler_params=params(56),
    )(var_index[None], pattern.T, view)
    return out.reshape(devices, cols + 1, rows, width)


def pick_kernel(cols, shares, table_ref, *rest):
    out_ref, table, notes, digits, wanted, held, sem, sems = rest[-8:]
    devices = digits.shape[0]
    each = cols // shares
    tell = pltpu.make_async_copy(table_ref.at[:, pl.ds(cols, 1)], notes, sem.at[0])
    load = pltpu.make_async_copy(table_ref.at[:, pl.ds(0, cols + 1)], table, sem.at[1])
    tell.start()
    load.start()
    tell.wait()
    for u in range(devices):
        note = notes[u, 0].astype(F32)
        digits[u : u + 1, :] = (note[:1] * DIGIT + note[1:2]).astype(jnp.int32)
    move = pltpu.make_async_copy(digits, wanted, sem.at[2])
    move.start()
    move.wait()
    load.wait()
    flat = table.reshape((devices * (cols + 1),) + table.shape[2:])
    sent = []
    for s in range(shares):

        @pl.loop(0, devices, unroll=8)
        def _(d):
            for j in range(each):
                held[s, d, j] = flat[wanted[d, s * each + j]]

        copy = pltpu.make_async_copy(held.at[s], out_ref.at[pl.ds(s * devices, devices)], sems.at[s])
        copy.start()
        sent.append(copy)
    for copy in sent:
        copy.wait()


def pick(table, cols, shares, after):
    devices, _, rows, width = table.shape
    each = cols // shares
    return pl.pallas_call(
        functools.partial(pick_kernel, cols, shares),
        in_specs=[HBM] + [HBM] * len(after),
        out_specs=HBM,
        out_shape=jax.ShapeDtypeStruct((shares * devices, each, rows, width), table.dtype),
        scratch_shapes=[
            pltpu.VMEM((devices, cols + 1, rows, width), table.dtype),
            pltpu.VMEM((devices, 1, rows, width), table.dtype),
            pltpu.VMEM((devices, width), jnp.int32),
            pltpu.SMEM((devices, width), jnp.int32),
            pltpu.VMEM((shares, devices, each, rows, width), table.dtype),
            pltpu.SemaphoreType.DMA((3,)),
            pltpu.SemaphoreType.DMA((shares,)),
        ],
        compiler_params=params(56),
    )(table, *after)


def near_kernel(info_ref, own_ref, p1_ref, p2_ref, p3_ref, blocks_ref, near_ref, turned_ref, start_ref):
    samp, rows, width = info_ref[0], own_ref.shape[0], own_ref.shape[1]
    for k, ref in enumerate((own_ref, p1_ref, p2_ref, p3_ref)):
        q = lax.rem(samp + 4 - k, 4)
        at = pl.multiple_of(q * rows, rows)
        x = ref[...]
        near_ref[0, pl.ds(at, rows), :] = x
        turned_ref[0, :, pl.ds(at, rows)] = x.T
    where_diag = info_ref[2 + pl.program_id(0)]
    start_ref[0, :width] = blocks_ref[0, where_diag]
    start_ref[0, width:] = blocks_ref[0, 1 - where_diag]


def near_panels(info, observed, received, blocks, each):
    rows, width = observed.shape[0], blocks.shape[-1]
    part = pl.BlockSpec((rows, width), lambda j, f: (0, j))
    return pl.pallas_call(
        near_kernel,
        grid_spec=pltpu.PrefetchScalarGridSpec(
            num_scalar_prefetch=1,
            grid=(each,),
            in_specs=[
                pl.BlockSpec((rows, width), lambda j, f: (0, f[1] + j)),
                part,
                part,
                part,
                pl.BlockSpec((1, 2, width, width), lambda j, f: (f[1] + j, 0, 0, 0)),
            ],
            out_specs=[
                pl.BlockSpec((1, 4 * rows, width), lambda j, f: (j, 0, 0)),
                pl.BlockSpec((1, width, 4 * rows), lambda j, f: (j, 0, 0)),
                pl.BlockSpec((1, 2 * width, width), lambda j, f: (j, 0, 0)),
            ],
        ),
        out_shape=[
            jax.ShapeDtypeStruct((each, 4 * rows, width), BF16),
            jax.ShapeDtypeStruct((each, width, 4 * rows), BF16),
            jax.ShapeDtypeStruct((each, 2 * width, width), F32),
        ],
        compiler_params=params(56),
        cost_estimate=cost(1 << 20, 10 << 20),
    )(info, observed, *received, blocks)


def shrink(v, level):
    return jnp.where(v > level, v - level, jnp.where(v < -level, v + level, 0.0))


def split3(g):
    hi = g.astype(BF16)
    rest = g - hi.astype(F32)
    mid = rest.astype(BF16)
    return hi, mid, (rest - mid.astype(F32)).astype(BF16)


def steps_kernel(info_ref, far_ref, near_ref, turned_ref, start_ref, diag_ref, out0_ref, out1_ref, obj_ref):
    count, total_rows, width = far_ref.shape
    eye = lax.broadcasted_iota(jnp.int32, (width, width), 0) == lax.broadcasted_iota(jnp.int32, (width, width), 1)
    each = range(count)
    grams = []
    for c in each:
        far = far_ref[c]
        both = jnp.concatenate([near_ref[c], far], axis=1)
        top = jnp.dot(turned_ref[c], both, preferred_element_type=F32)
        low = lax.dot_general(far, both, (((0,), (0,)), ((), ())), preferred_element_type=F32)
        grams.append(split3(jnp.concatenate([top, low], axis=0)))
    db = [jnp.where(eye, 0.0, start_ref[c, :width]) for c in each]
    ob = [start_ref[c, width:] for c in each]
    dv = [diag_ref[pl.ds(info_ref[1] + c, 1), :] for c in each]
    lane = lax.broadcasted_iota(jnp.int32, (1, width), 1)
    total = jnp.zeros((1, width), F32)
    for i in range(STEPS):
        w = [
            jnp.concatenate([jnp.where(eye, jnp.broadcast_to(dv[c], (width, width)), db[c]), ob[c]], axis=0).astype(BF16)
            for c in each
        ]
        g = [sum(jnp.dot(p, w[c], preferred_element_type=F32) for p in reversed(grams[c])) for c in each]
        part = jnp.zeros((1, width), F32)
        for c in each:
            fit = jnp.sum(w[c].astype(F32) * g[c], axis=0, keepdims=True) / (2.0 * total_rows)
            size = jnp.sum(jnp.abs(db[c]) + jnp.abs(ob[c]), axis=0, keepdims=True)
            part = part + (fit - jnp.log(dv[c]) + PENALTY * size)
        total = jnp.where(lane == i, jnp.sum(part, axis=1, keepdims=True), total)
        for c in each:
            gd, go = g[c][:width] / total_rows, g[c][width:] / total_rows
            along = jnp.sum(jnp.where(eye, gd, 0.0), axis=0, keepdims=True)
            db[c] = jnp.where(eye, 0.0, shrink(db[c] - STEP_LENGTH * gd, STEP_LENGTH * PENALTY))
            ob[c] = shrink(ob[c] - STEP_LENGTH * go, STEP_LENGTH * PENALTY)
            m = dv[c] - STEP_LENGTH * along
            dv[c] = 0.5 * (m + jnp.sqrt(m * m + 4.0 * STEP_LENGTH))
    obj_ref[...] = total
    for c in each:
        where_diag = info_ref[2 + c]
        full = jnp.where(eye, jnp.broadcast_to(dv[c], (width, width)), db[c])
        half = count // 2
        out_ref = out0_ref if c < half else out1_ref
        out_ref[c % half, where_diag] = full.astype(out_ref.dtype)
        out_ref[c % half, 1 - where_diag] = ob[c].astype(out_ref.dtype)


def iterate(info, far, near, turned, start, diag_rows):
    count, width = far.shape[0], far.shape[2]
    return pl.pallas_call(
        steps_kernel,
        in_specs=[pl.BlockSpec(memory_space=pltpu.SMEM)] + [VMEM] * 5,
        out_specs=[VMEM] * 3,
        out_shape=[
            jax.ShapeDtypeStruct((count // 2, 2, width, width), BF16),
            jax.ShapeDtypeStruct((count // 2, 2, width, width), BF16),
            jax.ShapeDtypeStruct((1, width), F32),
        ],
        compiler_params=params(24),
        cost_estimate=cost(count << 29, 4 << 20),
    )(info, far, near, turned, start, diag_rows)


def put(which_ref, out_ref, diag_ref, at, column, block):
    width = block.shape[-1]
    eye = lax.broadcasted_iota(jnp.int32, (width, width), 0) == lax.broadcasted_iota(jnp.int32, (width, width), 1)
    where_diag = which_ref[column]
    full = block[where_diag].astype(F32)
    diag_ref[pl.ds(column, 1), :] = jnp.sum(jnp.where(eye, full, 0.0), axis=0, keepdims=True)
    out_ref[at + (where_diag,)] = jnp.where(eye, 0.0, full)
    out_ref[at + (1 - where_diag,)] = block[1 - where_diag].astype(F32)


def first_places_kernel(samp_ref, which_ref, own0, own1, one0, one1, three0, three1, out_ref, diag_ref):
    @pl.when(pl.program_id(0) == 0)
    def _():
        diag_ref[...] = jnp.zeros_like(diag_ref)

    block = own0.shape[0]
    half = pl.num_programs(0) * block
    for k, refs in ((0, (own0, own1)), (1, (one0, one1)), (3, (three0, three1))):
        q = lax.rem(samp_ref[0] + 4 - k, 4)
        for h, ref in enumerate(refs):
            for c in range(block):
                put(which_ref, out_ref, diag_ref, (q, h, c), (q * 2 + h) * half + pl.program_id(0) * block + c, ref.at[c])


def last_places_kernel(scale, samp_ref, which_ref, low_ref, high_ref, _, old_diag_ref, terms_ref, out_ref, diag_ref, objective_ref):
    @pl.when(pl.program_id(0) == 0)
    def _():
        diag_ref[...] = old_diag_ref[...]
        total = jnp.sum(terms_ref[...], axis=0)
        lane = lax.broadcasted_iota(jnp.int32, total.shape, 1)
        for i in range(STEPS):
            objective_ref[i] = jnp.sum(jnp.where(lane == i, total, 0.0)) * scale

    block = low_ref.shape[0]
    half = pl.num_programs(0) * block
    for h, ref in enumerate((low_ref, high_ref)):
        for c in range(block):
            column = (lax.rem(samp_ref[0] + 2, 4) * 2 + h) * half + pl.program_id(0) * block + c
            put(which_ref, out_ref, diag_ref, (0, h, c), column, ref.at[c])


def place_first(samp, which, own, one, three):
    half, tail = own[0].shape[0], own[0].shape[1:]
    zeros = (0,) * len(tail)
    block = 2
    part = pl.BlockSpec((block,) + tail, lambda j, f, w: (j,) + zeros)
    return pl.pallas_call(
        first_places_kernel,
        grid_spec=pltpu.PrefetchScalarGridSpec(
            num_scalar_prefetch=2,
            grid=(half // block,),
            in_specs=[part] * 6,
            out_specs=[
                pl.BlockSpec((4, 2, block) + tail, lambda j, f, w: (0, 0, j) + zeros),
                pl.BlockSpec((8 * half, tail[-1]), lambda j, f, w: (0, 0)),
            ],
        ),
        out_shape=[jax.ShapeDtypeStruct((4, 2, half) + tail, F32), jax.ShapeDtypeStruct((8 * half, tail[-1]), F32)],
        compiler_params=params(24),
        cost_estimate=cost(1 << 20, 6 << 20),
    )(samp[None], which, *own, *one, *three)


def place_last(samp, which, low, high, out, diagonal, terms, scale):
    half, tail = low.shape[0], low.shape[1:]
    zeros = (0,) * len(tail)
    block = 2
    shape = (4, 2, half) + tail
    part = pl.BlockSpec((block,) + tail, lambda j, f, w: (j,) + zeros)
    diag = pl.BlockSpec(diagonal.shape, lambda j, f, w: (0, 0))
    out, diagonal, objective = pl.pallas_call(
        functools.partial(last_places_kernel, scale),
        grid_spec=pltpu.PrefetchScalarGridSpec(
            num_scalar_prefetch=2,
            grid=(half // block,),
            in_specs=[part, part, ANY, diag, pl.BlockSpec(terms.shape, lambda j, f, w: (0, 0, 0))],
            out_specs=[
                pl.BlockSpec((1, 2, block) + tail, lambda j, f, w: (lax.rem(f[0] + 2, 4), 0, j) + zeros),
                diag,
                pl.BlockSpec(memory_space=pltpu.SMEM),
            ],
        ),
        out_shape=[
            jax.ShapeDtypeStruct(shape, F32),
            jax.ShapeDtypeStruct(diagonal.shape, F32),
            jax.ShapeDtypeStruct((STEPS,), F32),
        ],
        input_output_aliases={4: 0},
        compiler_params=params(16),
        cost_estimate=cost(1 << 20, 2 << 20),
    )(samp[None], which, low, high, out.reshape(shape), diagonal, terms)
    return out.reshape((8 * half,) + tail), diagonal.reshape(-1), objective


def body(observed, blocks, diagonal, pattern):
    cols, _, width, _ = blocks.shape
    rows = observed.shape[0]
    devices = lax.axis_size(VAR)
    shares = lax.axis_size("samp")
    each = cols // shares
    total_rows = rows * shares
    samp = lax.axis_index("samp").astype(jnp.int32)
    var_index = lax.axis_index(VAR).astype(jnp.int32)

    pieces = cut(var_index, pattern, observed, devices, cols, width)
    panel = each * width
    received = [shift(lax.dynamic_slice_in_dim(observed, lax.rem(samp + k, shares) * panel, panel, 1), "samp", k) for k in (1, 2, 3)]
    table = lax.all_to_all(pieces, VAR, split_axis=0, concat_axis=0, tiled=True)
    start = samp * each
    columns = var_index * cols + jnp.arange(cols, dtype=jnp.int32)
    which = jnp.where(pattern[:, 0] == columns, 0, 1).astype(jnp.int32)
    info = jnp.concatenate([jnp.stack([samp, start]), lax.dynamic_slice_in_dim(which, start, each, 0)])
    near, turned, begin = near_panels(info, observed, received, blocks, each)
    outgoing = pick(table, cols, shares, (near, turned, begin))
    far = lax.all_to_all(outgoing, ALL, split_axis=0, concat_axis=0, tiled=True)

    diag_rows = diagonal.reshape(cols, width)
    far = far.transpose(1, 0, 2, 3).reshape(each, total_rows, width)
    *new, obj = iterate(info, far, near, turned, begin, diag_rows)
    one = [shift(x, "samp", 1) for x in new]
    three = [shift(x, "samp", 3) for x in new]
    two = [shift(one[0], "samp", 1), shift(three[1], "samp", 3)]
    terms = jnp.broadcast_to(obj[None], (shares * devices, 1, width))
    terms = lax.all_to_all(terms, ALL, split_axis=0, concat_axis=0, tiled=True)
    placed, diag = place_first(samp, which, new, one, three)
    return place_last(samp, which, *two, placed, diag, terms, 1.0 / (cols * devices * width))


def solution(mesh):
    torus = Mesh(mesh.devices.reshape(mesh.shape["samp"], 4, 8, 2), ALL)
    placed = (P("samp", VAR), P(VAR, None, None, None), P(VAR), P(VAR, None))
    return jax.shard_map(
        body,
        mesh=torus,
        in_specs=placed,
        out_specs=(P(VAR, None, None, None), P(VAR), P()),
        check_vma=False,
    )
```

```python
import functools

import jax
import jax.numpy as jnp
from jax import lax
from jax.experimental import pallas as pl
from jax.experimental.pallas import tpu as pltpu
from jax.sharding import Mesh
from jax.sharding import PartitionSpec as P

STEPS = 2
STEP_LENGTH = 0.5
PENALTY = 0.5
DIGIT = 64
VAR = ("var_0", "var_1", "var_2")
ALL = ("samp", "var_0", "var_1", "var_2")
F32 = jnp.float32
BF16 = jnp.bfloat16
VMEM = pl.BlockSpec(memory_space=pltpu.VMEM)
ANY = pl.BlockSpec(memory_space=pl.ANY)
HBM = pl.BlockSpec(memory_space=pltpu.HBM)


def params(mib):
    return pltpu.CompilerParams(vmem_limit_bytes=mib << 20)


def cost(flops, bytes_accessed):
    return pl.CostEstimate(flops=flops, bytes_accessed=bytes_accessed, transcendentals=0)


def shift(x, axis, k):
    n = lax.axis_size(axis)
    return lax.ppermute(x, axis, [(i, (i + k) % n) for i in range(n)])


def cut_kernel(cols, chunks, at_ref, pattern_ref, data_ref, out_ref, held, cutting, in_sems, out_sems):
    tiles, _, halves, rows, width = data_ref.shape
    each = tiles // chunks
    loads = [
        pltpu.make_async_copy(data_ref.at[pl.ds(i * each, each)], held.at[pl.ds(i * each, each)], in_sems.at[i])
        for i in range(chunks)
    ]
    for load in loads:
        load.start()
    first, second = pattern_ref[0:1, :], pattern_ref[1:2, :]
    lane = lax.broadcasted_iota(jnp.int32, first.shape, 1)
    block = jnp.where(first == at_ref[0] * cols + lane, second, first)
    place = block + lax.div(block, cols)
    digits = jnp.concatenate([lax.div(place, DIGIT), lax.rem(place, DIGIT)], axis=0).astype(F32)
    wide = jnp.concatenate([digits, jnp.zeros((rows - 2, cols), F32)], axis=0)
    wide = jnp.concatenate([wide, jnp.zeros((rows, width - cols), F32)], axis=1).astype(out_ref.dtype)
    for t in range(tiles):
        for h in range(halves):
            cutting[t, h, cols] = wide
    stores = []
    for i, load in enumerate(loads):
        load.wait()

        @pl.loop(i * each, (i + 1) * each)
        def _(t):
            for b in range(cols):
                for h in range(halves):
                    cutting[t, h, b] = held[t, b, h]

        store = pltpu.make_async_copy(cutting.at[pl.ds(i * each, each)], out_ref.at[pl.ds(i * each, each)], out_sems.at[i])
        store.start()
        stores.append(store)
    for store in stores:
        store.wait()


def cut(var_index, pattern, data, devices, cols, width):
    rows = data.shape[0] // devices
    tiles = devices // 2
    view = data.reshape(tiles, 2 * rows, cols, width).transpose(0, 2, 1, 3).reshape(tiles, cols, 2, rows, width)
    chunks = 8
    shape = (tiles, 2, cols + 1, rows, width)
    out = pl.pallas_call(
        functools.partial(cut_kernel, cols, chunks),
        in_specs=[pl.BlockSpec(memory_space=pltpu.SMEM), VMEM, HBM],
        out_specs=HBM,
        out_shape=jax.ShapeDtypeStruct(shape, data.dtype),
        scratch_shapes=[
            pltpu.VMEM(view.shape, data.dtype),
            pltpu.VMEM(shape, data.dtype),
            pltpu.SemaphoreType.DMA((chunks,)),
            pltpu.SemaphoreType.DMA((chunks,)),
        ],
        compiler_params=params(56),
    )(var_index[None], pattern.T, view)
    return out.reshape(devices, cols + 1, rows, width)


def pick_kernel(cols, shares, table_ref, *rest):
    out_ref, table, notes, digits, wanted, held, sem, sems = rest[-8:]
    devices = digits.shape[0]
    each = cols // shares
    tell = pltpu.make_async_copy(table_ref.at[:, pl.ds(cols, 1)], notes, sem.at[0])
    load = pltpu.make_async_copy(table_ref.at[:, pl.ds(0, cols + 1)], table, sem.at[1])
    tell.start()
    load.start()
    tell.wait()
    for u in range(devices):
        note = notes[u, 0].astype(F32)
        digits[u : u + 1, :] = (note[:1] * DIGIT + note[1:2]).astype(jnp.int32)
    move = pltpu.make_async_copy(digits, wanted, sem.at[2])
    move.start()
    move.wait()
    load.wait()
    flat = table.reshape((devices * (cols + 1),) + table.shape[2:])
    sent = []
    for s in range(shares):

        @pl.loop(0, devices, unroll=8)
        def _(d):
            for j in range(each):
                held[s, d, j] = flat[wanted[d, s * each + j]]

        copy = pltpu.make_async_copy(held.at[s], out_ref.at[pl.ds(s * devices, devices)], sems.at[s])
        copy.start()
        sent.append(copy)
    for copy in sent:
        copy.wait()


def pick(table, cols, shares, after):
    devices, _, rows, width = table.shape
    each = cols // shares
    return pl.pallas_call(
        functools.partial(pick_kernel, cols, shares),
        in_specs=[HBM] + [HBM] * len(after),
        out_specs=HBM,
        out_shape=jax.ShapeDtypeStruct((shares * devices, each, rows, width), table.dtype),
        scratch_shapes=[
            pltpu.VMEM((devices, cols + 1, rows, width), table.dtype),
            pltpu.VMEM((devices, 1, rows, width), table.dtype),
            pltpu.VMEM((devices, width), jnp.int32),
            pltpu.SMEM((devices, width), jnp.int32),
            pltpu.VMEM((shares, devices, each, rows, width), table.dtype),
            pltpu.SemaphoreType.DMA((3,)),
            pltpu.SemaphoreType.DMA((shares,)),
        ],
        compiler_params=params(56),
    )(table, *after)


def near_kernel(info_ref, own_ref, p1_ref, p2_ref, p3_ref, blocks_ref, near_ref, turned_ref, start_ref):
    samp, rows, width = info_ref[0], own_ref.shape[0], own_ref.shape[1]
    for k, ref in enumerate((own_ref, p1_ref, p2_ref, p3_ref)):
        q = lax.rem(samp + 4 - k, 4)
        at = pl.multiple_of(q * rows, rows)
        x = ref[...]
        near_ref[0, pl.ds(at, rows), :] = x
        turned_ref[0, :, pl.ds(at, rows)] = x.T
    where_diag = info_ref[2 + pl.program_id(0)]
    start_ref[0, :width] = blocks_ref[0, where_diag]
    start_ref[0, width:] = blocks_ref[0, 1 - where_diag]


def near_panels(info, observed, received, blocks, each):
    rows, width = observed.shape[0], blocks.shape[-1]
    part = pl.BlockSpec((rows, width), lambda j, f: (0, j))
    return pl.pallas_call(
        near_kernel,
        grid_spec=pltpu.PrefetchScalarGridSpec(
            num_scalar_prefetch=1,
            grid=(each,),
            in_specs=[
                pl.BlockSpec((rows, width), lambda j, f: (0, f[1] + j)),
                part,
                part,
                part,
                pl.BlockSpec((1, 2, width, width), lambda j, f: (f[1] + j, 0, 0, 0)),
            ],
            out_specs=[
                pl.BlockSpec((1, 4 * rows, width), lambda j, f: (j, 0, 0)),
                pl.BlockSpec((1, width, 4 * rows), lambda j, f: (j, 0, 0)),
                pl.BlockSpec((1, 2 * width, width), lambda j, f: (j, 0, 0)),
            ],
        ),
        out_shape=[
            jax.ShapeDtypeStruct((each, 4 * rows, width), BF16),
            jax.ShapeDtypeStruct((each, width, 4 * rows), BF16),
            jax.ShapeDtypeStruct((each, 2 * width, width), F32),
        ],
        compiler_params=params(56),
        cost_estimate=cost(1 << 20, 10 << 20),
    )(info, observed, *received, blocks)


def shrink(v, level):
    return jnp.where(v > level, v - level, jnp.where(v < -level, v + level, 0.0))


def split3(g):
    hi = g.astype(BF16)
    rest = g - hi.astype(F32)
    mid = rest.astype(BF16)
    return hi, mid, (rest - mid.astype(F32)).astype(BF16)


def steps_kernel(info_ref, far_ref, near_ref, turned_ref, start_ref, diag_ref, out0_ref, out1_ref, obj_ref):
    count, total_rows, width = far_ref.shape
    eye = lax.broadcasted_iota(jnp.int32, (width, width), 0) == lax.broadcasted_iota(jnp.int32, (width, width), 1)
    each = range(count)
    grams = []
    for c in each:
        far = far_ref[c]
        both = jnp.concatenate([near_ref[c], far], axis=1)
        top = jnp.dot(turned_ref[c], both, preferred_element_type=F32)
        low = lax.dot_general(far, both, (((0,), (0,)), ((), ())), preferred_element_type=F32)
        grams.append(split3(jnp.concatenate([top, low], axis=0)))
    db = [jnp.where(eye, 0.0, start_ref[c, :width]) for c in each]
    ob = [start_ref[c, width:] for c in each]
    dv = [diag_ref[pl.ds(info_ref[1] + c, 1), :] for c in each]
    lane = lax.broadcasted_iota(jnp.int32, (1, width), 1)
    total = jnp.zeros((1, width), F32)
    for i in range(STEPS):
        w = [
            jnp.concatenate([jnp.where(eye, jnp.broadcast_to(dv[c], (width, width)), db[c]), ob[c]], axis=0).astype(BF16)
            for c in each
        ]
        g = [sum(jnp.dot(p, w[c], preferred_element_type=F32) for p in reversed(grams[c])) for c in each]
        part = jnp.zeros((1, width), F32)
        for c in each:
            fit = jnp.sum(w[c].astype(F32) * g[c], axis=0, keepdims=True) / (2.0 * total_rows)
            size = jnp.sum(jnp.abs(db[c]) + jnp.abs(ob[c]), axis=0, keepdims=True)
            part = part + (fit - jnp.log(dv[c]) + PENALTY * size)
        total = jnp.where(lane == i, jnp.sum(part, axis=1, keepdims=True), total)
        for c in each:
            gd, go = g[c][:width] / total_rows, g[c][width:] / total_rows
            along = jnp.sum(jnp.where(eye, gd, 0.0), axis=0, keepdims=True)
            db[c] = jnp.where(eye, 0.0, shrink(db[c] - STEP_LENGTH * gd, STEP_LENGTH * PENALTY))
            ob[c] = shrink(ob[c] - STEP_LENGTH * go, STEP_LENGTH * PENALTY)
            m = dv[c] - STEP_LENGTH * along
            dv[c] = 0.5 * (m + jnp.sqrt(m * m + 4.0 * STEP_LENGTH))
    obj_ref[...] = total
    for c in each:
        where_diag = info_ref[2 + c]
        full = jnp.where(eye, jnp.broadcast_to(dv[c], (width, width)), db[c])
        half = count // 2
        out_ref = out0_ref if c < half else out1_ref
        out_ref[c % half, where_diag] = full.astype(out_ref.dtype)
        out_ref[c % half, 1 - where_diag] = ob[c].astype(out_ref.dtype)


def iterate(info, far, near, turned, start, diag_rows):
    count, width = far.shape[0], far.shape[2]
    return pl.pallas_call(
        steps_kernel,
        in_specs=[pl.BlockSpec(memory_space=pltpu.SMEM)] + [VMEM] * 5,
        out_specs=[VMEM] * 3,
        out_shape=[
            jax.ShapeDtypeStruct((count // 2, 2, width, width), BF16),
            jax.ShapeDtypeStruct((count // 2, 2, width, width), BF16),
            jax.ShapeDtypeStruct((1, width), F32),
        ],
        compiler_params=params(24),
        cost_estimate=cost(count << 29, 4 << 20),
    )(info, far, near, turned, start, diag_rows)


def put(which_ref, out_ref, diag_ref, at, column, block):
    width = block.shape[-1]
    eye = lax.broadcasted_iota(jnp.int32, (width, width), 0) == lax.broadcasted_iota(jnp.int32, (width, width), 1)
    where_diag = which_ref[column]
    full = block[where_diag].astype(F32)
    diag_ref[pl.ds(column, 1), :] = jnp.sum(jnp.where(eye, full, 0.0), axis=0, keepdims=True)
    out_ref[at + (where_diag,)] = jnp.where(eye, 0.0, full)
    out_ref[at + (1 - where_diag,)] = block[1 - where_diag].astype(F32)


def first_places_kernel(samp_ref, which_ref, own0, own1, one0, one1, three0, three1, out_ref, diag_ref):
    @pl.when(pl.program_id(0) == 0)
    def _():
        diag_ref[...] = jnp.zeros_like(diag_ref)

    block = own0.shape[0]
    half = pl.num_programs(0) * block
    for k, refs in ((0, (own0, own1)), (1, (one0, one1)), (3, (three0, three1))):
        q = lax.rem(samp_ref[0] + 4 - k, 4)
        for h, ref in enumerate(refs):
            for c in range(block):
                put(which_ref, out_ref, diag_ref, (q, h, c), (q * 2 + h) * half + pl.program_id(0) * block + c, ref.at[c])


def last_places_kernel(samp_ref, which_ref, low_ref, high_ref, _, old_diag_ref, out_ref, diag_ref):
    @pl.when(pl.program_id(0) == 0)
    def _():
        diag_ref[...] = old_diag_ref[...]

    block = low_ref.shape[0]
    half = pl.num_programs(0) * block
    for h, ref in enumerate((low_ref, high_ref)):
        for c in range(block):
            column = (lax.rem(samp_ref[0] + 2, 4) * 2 + h) * half + pl.program_id(0) * block + c
            put(which_ref, out_ref, diag_ref, (0, h, c), column, ref.at[c])


def place_first(samp, which, own, one, three):
    half, tail = own[0].shape[0], own[0].shape[1:]
    zeros = (0,) * len(tail)
    block = 2
    part = pl.BlockSpec((block,) + tail, lambda j, f, w: (j,) + zeros)
    return pl.pallas_call(
        first_places_kernel,
        grid_spec=pltpu.PrefetchScalarGridSpec(
            num_scalar_prefetch=2,
            grid=(half // block,),
            in_specs=[part] * 6,
            out_specs=[
                pl.BlockSpec((4, 2, block) + tail, lambda j, f, w: (0, 0, j) + zeros),
                pl.BlockSpec((8 * half, tail[-1]), lambda j, f, w: (0, 0)),
            ],
        ),
        out_shape=[jax.ShapeDtypeStruct((4, 2, half) + tail, F32), jax.ShapeDtypeStruct((8 * half, tail[-1]), F32)],
        compiler_params=params(24),
        cost_estimate=cost(1 << 20, 6 << 20),
    )(samp[None], which, *own, *one, *three)


def place_last(samp, which, low, high, out, diagonal):
    half, tail = low.shape[0], low.shape[1:]
    zeros = (0,) * len(tail)
    block = 2
    shape = (4, 2, half) + tail
    part = pl.BlockSpec((block,) + tail, lambda j, f, w: (j,) + zeros)
    diag = pl.BlockSpec(diagonal.shape, lambda j, f, w: (0, 0))
    out, diagonal = pl.pallas_call(
        last_places_kernel,
        grid_spec=pltpu.PrefetchScalarGridSpec(
            num_scalar_prefetch=2,
            grid=(half // block,),
            in_specs=[part, part, ANY, diag],
            out_specs=[
                pl.BlockSpec((1, 2, block) + tail, lambda j, f, w: (lax.rem(f[0] + 2, 4), 0, j) + zeros),
                diag,
            ],
        ),
        out_shape=[
            jax.ShapeDtypeStruct(shape, F32),
            jax.ShapeDtypeStruct(diagonal.shape, F32),
        ],
        input_output_aliases={4: 0},
        compiler_params=params(16),
        cost_estimate=cost(1 << 20, 2 << 20),
    )(samp[None], which, low, high, out.reshape(shape), diagonal)
    return out.reshape((8 * half,) + tail), diagonal.reshape(-1)


def body(observed, blocks, diagonal, pattern):
    cols, _, width, _ = blocks.shape
    rows = observed.shape[0]
    devices = lax.axis_size(VAR)
    shares = lax.axis_size("samp")
    each = cols // shares
    total_rows = rows * shares
    samp = lax.axis_index("samp").astype(jnp.int32)
    var_index = lax.axis_index(VAR).astype(jnp.int32)

    pieces = cut(var_index, pattern, observed, devices, cols, width)
    panel = each * width
    received = [shift(lax.dynamic_slice_in_dim(observed, lax.rem(samp + k, shares) * panel, panel, 1), "samp", k) for k in (1, 2, 3)]
    table = lax.all_to_all(pieces, VAR, split_axis=0, concat_axis=0, tiled=True)
    start = samp * each
    columns = var_index * cols + jnp.arange(cols, dtype=jnp.int32)
    which = jnp.where(pattern[:, 0] == columns, 0, 1).astype(jnp.int32)
    info = jnp.concatenate([jnp.stack([samp, start]), lax.dynamic_slice_in_dim(which, start, each, 0)])
    near, turned, begin = near_panels(info, observed, received, blocks, each)
    outgoing = pick(table, cols, shares, (near, turned, begin))
    far = lax.all_to_all(outgoing, ALL, split_axis=0, concat_axis=0, tiled=True)

    diag_rows = diagonal.reshape(cols, width)
    far = far.transpose(1, 0, 2, 3).reshape(each, total_rows, width)
    *new, obj = iterate(info, far, near, turned, begin, diag_rows)
    one = [shift(x, "samp", 1) for x in new]
    three = [shift(x, "samp", 3) for x in new]
    two = [shift(one[0], "samp", 1), shift(three[1], "samp", 3)]
    terms = jnp.broadcast_to(obj[None], (shares * devices, 1, width))
    terms = lax.all_to_all(terms, ALL, split_axis=0, concat_axis=0, tiled=True)
    placed, diag = place_first(samp, which, new, one, three)
    terms, diag = lax.optimization_barrier((terms, diag))
    terms = jnp.sum(terms, axis=(0, 1))
    new_blocks, new_diagonal = place_last(samp, which, *two, placed, diag)
    return (new_blocks, new_diagonal, terms[:STEPS] / (cols * devices * width))


def solution(mesh):
    torus = Mesh(mesh.devices.reshape(mesh.shape["samp"], 4, 8, 2), ALL)
    placed = (P("samp", VAR), P(VAR, None, None, None), P(VAR), P(VAR, None))
    return jax.shard_map(
        body,
        mesh=torus,
        in_specs=placed,
        out_specs=(P(VAR, None, None, None), P(VAR), P()),
        check_vma=False,
    )
```

```python
import functools

import jax
import jax.numpy as jnp
from jax import lax
from jax.experimental import pallas as pl
from jax.experimental.pallas import tpu as pltpu
from jax.sharding import Mesh
from jax.sharding import PartitionSpec as P

STEPS = 2
STEP_LENGTH = 0.5
PENALTY = 0.5
DIGIT = 64
VAR = ("var_0", "var_1", "var_2")
ALL = ("samp", "var_0", "var_1", "var_2")
F32 = jnp.float32
BF16 = jnp.bfloat16
VMEM = pl.BlockSpec(memory_space=pltpu.VMEM)
ANY = pl.BlockSpec(memory_space=pl.ANY)
HBM = pl.BlockSpec(memory_space=pltpu.HBM)


def params(mib):
    return pltpu.CompilerParams(vmem_limit_bytes=mib << 20)


def cost(flops, bytes_accessed):
    return pl.CostEstimate(flops=flops, bytes_accessed=bytes_accessed, transcendentals=0)


def shift(x, axis, k):
    n = lax.axis_size(axis)
    return lax.ppermute(x, axis, [(i, (i + k) % n) for i in range(n)])


def cut_kernel(cols, chunks, at_ref, pattern_ref, data_ref, out_ref, held, cutting, in_sems, out_sems):
    tiles, _, halves, rows, width = data_ref.shape
    each = tiles // chunks
    loads = [
        pltpu.make_async_copy(data_ref.at[pl.ds(i * each, each)], held.at[pl.ds(i * each, each)], in_sems.at[i])
        for i in range(chunks)
    ]
    for load in loads:
        load.start()
    first, second = pattern_ref[0:1, :], pattern_ref[1:2, :]
    lane = lax.broadcasted_iota(jnp.int32, first.shape, 1)
    block = jnp.where(first == at_ref[0] * cols + lane, second, first)
    place = block + lax.div(block, cols)
    digits = jnp.concatenate([lax.div(place, DIGIT), lax.rem(place, DIGIT)], axis=0).astype(F32)
    wide = jnp.concatenate([digits, jnp.zeros((rows - 2, cols), F32)], axis=0)
    wide = jnp.concatenate([wide, jnp.zeros((rows, width - cols), F32)], axis=1).astype(out_ref.dtype)
    for t in range(tiles):
        for h in range(halves):
            cutting[t, h, cols] = wide
    stores = []
    for i, load in enumerate(loads):
        load.wait()

        @pl.loop(i * each, (i + 1) * each)
        def _(t):
            for b in range(cols):
                for h in range(halves):
                    cutting[t, h, b] = held[t, b, h]

        store = pltpu.make_async_copy(cutting.at[pl.ds(i * each, each)], out_ref.at[pl.ds(i * each, each)], out_sems.at[i])
        store.start()
        stores.append(store)
    for store in stores:
        store.wait()


def cut(var_index, pattern, data, devices, cols, width):
    rows = data.shape[0] // devices
    tiles = devices // 2
    view = data.reshape(tiles, 2 * rows, cols, width).transpose(0, 2, 1, 3).reshape(tiles, cols, 2, rows, width)
    chunks = 4
    shape = (tiles, 2, cols + 1, rows, width)
    out = pl.pallas_call(
        functools.partial(cut_kernel, cols, chunks),
        in_specs=[pl.BlockSpec(memory_space=pltpu.SMEM), VMEM, HBM],
        out_specs=HBM,
        out_shape=jax.ShapeDtypeStruct(shape, data.dtype),
        scratch_shapes=[
            pltpu.VMEM(view.shape, data.dtype),
            pltpu.VMEM(shape, data.dtype),
            pltpu.SemaphoreType.DMA((chunks,)),
            pltpu.SemaphoreType.DMA((chunks,)),
        ],
        compiler_params=params(56),
    )(var_index[None], pattern.T, view)
    return out.reshape(devices, cols + 1, rows, width)


def pick_kernel(cols, shares, table_ref, *rest):
    out_ref, table, notes, digits, wanted, held, sem, sems = rest[-8:]
    devices = digits.shape[0]
    each = cols // shares
    tell = pltpu.make_async_copy(table_ref.at[:, pl.ds(cols, 1)], notes, sem.at[0])
    load = pltpu.make_async_copy(table_ref.at[:, pl.ds(0, cols + 1)], table, sem.at[1])
    tell.start()
    load.start()
    tell.wait()
    for u in range(devices):
        note = notes[u, 0].astype(F32)
        digits[u : u + 1, :] = (note[:1] * DIGIT + note[1:2]).astype(jnp.int32)
    move = pltpu.make_async_copy(digits, wanted, sem.at[2])
    move.start()
    move.wait()
    load.wait()
    flat = table.reshape((devices * (cols + 1),) + table.shape[2:])
    sent = []
    for s in range(shares):

        @pl.loop(0, devices, unroll=8)
        def _(d):
            for j in range(each):
                held[s, d, j] = flat[wanted[d, s * each + j]]

        copy = pltpu.make_async_copy(held.at[s], out_ref.at[pl.ds(s * devices, devices)], sems.at[s])
        copy.start()
        sent.append(copy)
    for copy in sent:
        copy.wait()


def pick(table, cols, shares, after):
    devices, _, rows, width = table.shape
    each = cols // shares
    return pl.pallas_call(
        functools.partial(pick_kernel, cols, shares),
        in_specs=[HBM] + [HBM] * len(after),
        out_specs=HBM,
        out_shape=jax.ShapeDtypeStruct((shares * devices, each, rows, width), table.dtype),
        scratch_shapes=[
            pltpu.VMEM((devices, cols + 1, rows, width), table.dtype),
            pltpu.VMEM((devices, 1, rows, width), table.dtype),
            pltpu.VMEM((devices, width), jnp.int32),
            pltpu.SMEM((devices, width), jnp.int32),
            pltpu.VMEM((shares, devices, each, rows, width), table.dtype),
            pltpu.SemaphoreType.DMA((3,)),
            pltpu.SemaphoreType.DMA((shares,)),
        ],
        compiler_params=params(56),
    )(table, *after)


def near_kernel(info_ref, own_ref, p1_ref, p2_ref, p3_ref, blocks_ref, gram_ref, turned_ref, start_ref, near):
    samp, rows, width = info_ref[0], own_ref.shape[0], own_ref.shape[1]
    for k, ref in enumerate((own_ref, p1_ref, p2_ref, p3_ref)):
        q = lax.rem(samp + 4 - k, 4)
        at = pl.multiple_of(q * rows, rows)
        x = ref[...]
        near[pl.ds(at, rows), :] = x
        turned_ref[0, :, pl.ds(at, rows)] = x.T
    gram_ref[0] = jnp.dot(turned_ref[0], near[...], preferred_element_type=F32)
    where_diag = info_ref[2 + pl.program_id(0)]
    start_ref[0, :width] = blocks_ref[0, where_diag]
    start_ref[0, width:] = blocks_ref[0, 1 - where_diag]


def near_panels(info, observed, received, blocks, each):
    rows, width = observed.shape[0], blocks.shape[-1]
    part = pl.BlockSpec((rows, width), lambda j, f: (0, j))
    return pl.pallas_call(
        near_kernel,
        grid_spec=pltpu.PrefetchScalarGridSpec(
            num_scalar_prefetch=1,
            grid=(each,),
            in_specs=[
                pl.BlockSpec((rows, width), lambda j, f: (0, f[1] + j)),
                part,
                part,
                part,
                pl.BlockSpec((1, 2, width, width), lambda j, f: (f[1] + j, 0, 0, 0)),
            ],
            out_specs=[
                pl.BlockSpec((1, width, width), lambda j, f: (j, 0, 0)),
                pl.BlockSpec((1, width, 4 * rows), lambda j, f: (j, 0, 0)),
                pl.BlockSpec((1, 2 * width, width), lambda j, f: (j, 0, 0)),
            ],
            scratch_shapes=[pltpu.VMEM((4 * rows, width), BF16)],
        ),
        out_shape=[
            jax.ShapeDtypeStruct((each, width, width), F32),
            jax.ShapeDtypeStruct((each, width, 4 * rows), BF16),
            jax.ShapeDtypeStruct((each, 2 * width, width), F32),
        ],
        compiler_params=params(56),
        cost_estimate=cost(1 << 20, 10 << 20),
    )(info, observed, *received, blocks)


def shrink(v, level):
    return jnp.where(v > level, v - level, jnp.where(v < -level, v + level, 0.0))


def split3(g):
    hi = g.astype(BF16)
    rest = g - hi.astype(F32)
    mid = rest.astype(BF16)
    return hi, mid, (rest - mid.astype(F32)).astype(BF16)


def steps_kernel(info_ref, far_ref, near_ref, turned_ref, start_ref, diag_ref, out_ref, obj_ref):
    count, total_rows, width = far_ref.shape
    eye = lax.broadcasted_iota(jnp.int32, (width, width), 0) == lax.broadcasted_iota(jnp.int32, (width, width), 1)
    each = range(count)
    grams = []
    for c in each:
        far = far_ref[c]
        cross = jnp.dot(turned_ref[c], far, preferred_element_type=F32)
        own = lax.dot_general(far, far, (((0,), (0,)), ((), ())), preferred_element_type=F32)
        top = jnp.concatenate([near_ref[c], cross], axis=1)
        low = jnp.concatenate([cross.T, own], axis=1)
        grams.append(split3(jnp.concatenate([top, low], axis=0)))
    db = [jnp.where(eye, 0.0, start_ref[c, :width]) for c in each]
    ob = [start_ref[c, width:] for c in each]
    dv = [diag_ref[pl.ds(info_ref[1] + c, 1), :] for c in each]
    lane = lax.broadcasted_iota(jnp.int32, (1, width), 1)
    total = jnp.zeros((1, width), F32)
    for i in range(STEPS):
        w = [
            jnp.concatenate([jnp.where(eye, jnp.broadcast_to(dv[c], (width, width)), db[c]), ob[c]], axis=0).astype(BF16)
            for c in each
        ]
        g = [sum(jnp.dot(p, w[c], preferred_element_type=F32) for p in reversed(grams[c])) for c in each]
        part = jnp.zeros((1, width), F32)
        for c in each:
            fit = jnp.sum(w[c].astype(F32) * g[c], axis=0, keepdims=True) / (2.0 * total_rows)
            size = jnp.sum(jnp.abs(db[c]) + jnp.abs(ob[c]), axis=0, keepdims=True)
            part = part + (fit - jnp.log(dv[c]) + PENALTY * size)
        total = jnp.where(lane == i, jnp.sum(part, axis=1, keepdims=True), total)
        for c in each:
            gd, go = g[c][:width] / total_rows, g[c][width:] / total_rows
            along = jnp.sum(jnp.where(eye, gd, 0.0), axis=0, keepdims=True)
            db[c] = jnp.where(eye, 0.0, shrink(db[c] - STEP_LENGTH * gd, STEP_LENGTH * PENALTY))
            ob[c] = shrink(ob[c] - STEP_LENGTH * go, STEP_LENGTH * PENALTY)
            m = dv[c] - STEP_LENGTH * along
            dv[c] = 0.5 * (m + jnp.sqrt(m * m + 4.0 * STEP_LENGTH))
    obj_ref[...] = total
    for c in each:
        where_diag = info_ref[2 + c]
        full = jnp.where(eye, jnp.broadcast_to(dv[c], (width, width)), db[c])
        out_ref[c, where_diag] = full.astype(out_ref.dtype)
        out_ref[c, 1 - where_diag] = ob[c].astype(out_ref.dtype)


def iterate(info, far, near, turned, start, diag_rows):
    count, width = far.shape[0], far.shape[2]
    return pl.pallas_call(
        steps_kernel,
        in_specs=[pl.BlockSpec(memory_space=pltpu.SMEM)] + [VMEM] * 5,
        out_specs=[VMEM] * 2,
        out_shape=[
            jax.ShapeDtypeStruct((count, 2, width, width), BF16),
            jax.ShapeDtypeStruct((1, width), F32),
        ],
        compiler_params=params(24),
        cost_estimate=cost(count << 29, 4 << 20),
    )(info, far, near, turned, start, diag_rows)


def put(which_ref, out_ref, diag_ref, at, column, block):
    width = block.shape[-1]
    eye = lax.broadcasted_iota(jnp.int32, (width, width), 0) == lax.broadcasted_iota(jnp.int32, (width, width), 1)
    where_diag = which_ref[column]
    full = block[where_diag].astype(F32)
    diag_ref[pl.ds(column, 1), :] = jnp.sum(jnp.where(eye, full, 0.0), axis=0, keepdims=True)
    out_ref[at + (where_diag,)] = jnp.where(eye, 0.0, full)
    out_ref[at + (1 - where_diag,)] = block[1 - where_diag].astype(F32)


def first_places_kernel(samp_ref, which_ref, own_ref, one_ref, three_ref, out_ref, diag_ref):
    @pl.when(pl.program_id(0) == 0)
    def _():
        diag_ref[...] = jnp.zeros_like(diag_ref)

    block = own_ref.shape[0]
    for k, ref in ((0, own_ref), (1, one_ref), (3, three_ref)):
        q = lax.rem(samp_ref[0] + 4 - k, 4)
        for c in range(block):
            put(which_ref, out_ref, diag_ref, (q, c), (q * pl.num_programs(0) + pl.program_id(0)) * block + c, ref.at[c])


def last_places_kernel(samp_ref, which_ref, low_ref, high_ref, _, old_diag_ref, out_ref, diag_ref):
    @pl.when(pl.program_id(0) == 0)
    def _():
        diag_ref[...] = old_diag_ref[...]

    block = low_ref.shape[0]
    half = pl.num_programs(0) * block
    for h, ref in enumerate((low_ref, high_ref)):
        for c in range(block):
            column = (lax.rem(samp_ref[0] + 2, 4) * 2 + h) * half + pl.program_id(0) * block + c
            put(which_ref, out_ref, diag_ref, (0, h, c), column, ref.at[c])


def place_first(samp, which, own, one, three):
    count, tail = own.shape[0], own.shape[1:]
    zeros = (0,) * len(tail)
    block = 2
    part = pl.BlockSpec((block,) + tail, lambda j, f, w: (j,) + zeros)
    return pl.pallas_call(
        first_places_kernel,
        grid_spec=pltpu.PrefetchScalarGridSpec(
            num_scalar_prefetch=2,
            grid=(count // block,),
            in_specs=[part] * 3,
            out_specs=[
                pl.BlockSpec((4, block) + tail, lambda j, f, w: (0, j) + zeros),
                pl.BlockSpec((4 * count, tail[-1]), lambda j, f, w: (0, 0)),
            ],
        ),
        out_shape=[jax.ShapeDtypeStruct((4, count) + tail, F32), jax.ShapeDtypeStruct((4 * count, tail[-1]), F32)],
        compiler_params=params(24),
        cost_estimate=cost(1 << 20, 6 << 20),
    )(samp[None], which, own, one, three)


def place_last(samp, which, low, high, out, diagonal):
    half, tail = low.shape[0], low.shape[1:]
    zeros = (0,) * len(tail)
    block = 2
    shape = (4, 2, half) + tail
    part = pl.BlockSpec((block,) + tail, lambda j, f, w: (j,) + zeros)
    diag = pl.BlockSpec(diagonal.shape, lambda j, f, w: (0, 0))
    out, diagonal = pl.pallas_call(
        last_places_kernel,
        grid_spec=pltpu.PrefetchScalarGridSpec(
            num_scalar_prefetch=2,
            grid=(half // block,),
            in_specs=[part, part, ANY, diag],
            out_specs=[
                pl.BlockSpec((1, 2, block) + tail, lambda j, f, w: (lax.rem(f[0] + 2, 4), 0, j) + zeros),
                diag,
            ],
        ),
        out_shape=[
            jax.ShapeDtypeStruct(shape, F32),
            jax.ShapeDtypeStruct(diagonal.shape, F32),
        ],
        input_output_aliases={4: 0},
        compiler_params=params(16),
        cost_estimate=cost(1 << 20, 2 << 20),
    )(samp[None], which, low, high, out.reshape(shape), diagonal)
    return out.reshape((8 * half,) + tail), diagonal.reshape(-1)


def body(observed, blocks, diagonal, pattern):
    cols, _, width, _ = blocks.shape
    rows = observed.shape[0]
    devices = lax.axis_size(VAR)
    shares = lax.axis_size("samp")
    each = cols // shares
    total_rows = rows * shares
    samp = lax.axis_index("samp").astype(jnp.int32)
    var_index = lax.axis_index(VAR).astype(jnp.int32)

    pieces = cut(var_index, pattern, observed, devices, cols, width)
    panel = each * width
    received = [shift(lax.dynamic_slice_in_dim(observed, lax.rem(samp + k, shares) * panel, panel, 1), "samp", k) for k in (1, 2, 3)]
    table = lax.all_to_all(pieces, VAR, split_axis=0, concat_axis=0, tiled=True)
    start = samp * each
    columns = var_index * cols + jnp.arange(cols, dtype=jnp.int32)
    which = jnp.where(pattern[:, 0] == columns, 0, 1).astype(jnp.int32)
    info = jnp.concatenate([jnp.stack([samp, start]), lax.dynamic_slice_in_dim(which, start, each, 0)])
    near, turned, begin = near_panels(info, observed, received, blocks, each)
    outgoing = pick(table, cols, shares, (near, turned, begin))
    far = lax.all_to_all(outgoing, ALL, split_axis=0, concat_axis=0, tiled=True)

    diag_rows = diagonal.reshape(cols, width)
    far = far.transpose(1, 0, 2, 3).reshape(each, total_rows, width)
    new, obj = iterate(info, far, near, turned, begin, diag_rows)
    one, three = shift(new, "samp", 1), shift(new, "samp", 3)
    two = [shift(one[: each // 2], "samp", 1), shift(three[each // 2 :], "samp", 3)]
    terms = jnp.broadcast_to(obj[None], (shares * devices, 1, width))
    terms = lax.all_to_all(terms, ALL, split_axis=0, concat_axis=0, tiled=True)
    placed, diag = place_first(samp, which, new, one, three)
    terms, diag = lax.optimization_barrier((terms, diag))
    terms = jnp.sum(terms, axis=(0, 1))
    new_blocks, new_diagonal = place_last(samp, which, *two, placed, diag)
    return (new_blocks, new_diagonal, terms[:STEPS] / (cols * devices * width))


def solution(mesh):
    torus = Mesh(mesh.devices.reshape(mesh.shape["samp"], 4, 8, 2), ALL)
    placed = (P("samp", VAR), P(VAR, None, None, None), P(VAR), P(VAR, None))
    return jax.shard_map(
        body,
        mesh=torus,
        in_specs=placed,
        out_specs=(P(VAR, None, None, None), P(VAR), P()),
        check_vma=False,
    )
```

```python
import functools

import jax
import jax.numpy as jnp
from jax import lax
from jax.experimental import pallas as pl
from jax.experimental.pallas import tpu as pltpu
from jax.sharding import Mesh
from jax.sharding import PartitionSpec as P

STEPS = 2
STEP_LENGTH = 0.5
PENALTY = 0.5
DIGIT = 64
VAR = ("var_0", "var_1", "var_2")
ALL = ("samp", "var_0", "var_1", "var_2")
F32 = jnp.float32
BF16 = jnp.bfloat16
VMEM = pl.BlockSpec(memory_space=pltpu.VMEM)
ANY = pl.BlockSpec(memory_space=pl.ANY)
HBM = pl.BlockSpec(memory_space=pltpu.HBM)


def params(mib):
    return pltpu.CompilerParams(vmem_limit_bytes=mib << 20)


def cost(flops, bytes_accessed):
    return pl.CostEstimate(flops=flops, bytes_accessed=bytes_accessed, transcendentals=0)


def shift(x, axis, k):
    n = lax.axis_size(axis)
    return lax.ppermute(x, axis, [(i, (i + k) % n) for i in range(n)])


def cut_kernel(cols, chunks, at_ref, pattern_ref, data_ref, out_ref, held, cutting, in_sems, out_sems):
    tiles, _, halves, rows, width = data_ref.shape
    each = tiles // chunks
    loads = [
        pltpu.make_async_copy(data_ref.at[pl.ds(i * each, each)], held.at[pl.ds(i * each, each)], in_sems.at[i])
        for i in range(chunks)
    ]
    for load in loads:
        load.start()
    first, second = pattern_ref[0:1, :], pattern_ref[1:2, :]
    lane = lax.broadcasted_iota(jnp.int32, first.shape, 1)
    block = jnp.where(first == at_ref[0] * cols + lane, second, first)
    place = block + lax.div(block, cols)
    digits = jnp.concatenate([lax.div(place, DIGIT), lax.rem(place, DIGIT)], axis=0).astype(F32)
    wide = jnp.concatenate([digits, jnp.zeros((rows - 2, cols), F32)], axis=0)
    wide = jnp.concatenate([wide, jnp.zeros((rows, width - cols), F32)], axis=1).astype(out_ref.dtype)
    for t in range(tiles):
        for h in range(halves):
            cutting[t, h, cols] = wide
    stores = []
    for i, load in enumerate(loads):
        load.wait()

        @pl.loop(i * each, (i + 1) * each)
        def _(t):
            for b in range(cols):
                for h in range(halves):
                    cutting[t, h, b] = held[t, b, h]

        store = pltpu.make_async_copy(cutting.at[pl.ds(i * each, each)], out_ref.at[pl.ds(i * each, each)], out_sems.at[i])
        store.start()
        stores.append(store)
    for store in stores:
        store.wait()


def cut(var_index, pattern, data, devices, cols, width):
    rows = data.shape[0] // devices
    tiles = devices // 2
    view = data.reshape(tiles, 2 * rows, cols, width).transpose(0, 2, 1, 3).reshape(tiles, cols, 2, rows, width)
    chunks = 8
    shape = (tiles, 2, cols + 1, rows, width)
    out = pl.pallas_call(
        functools.partial(cut_kernel, cols, chunks),
        in_specs=[pl.BlockSpec(memory_space=pltpu.SMEM), VMEM, HBM],
        out_specs=HBM,
        out_shape=jax.ShapeDtypeStruct(shape, data.dtype),
        scratch_shapes=[
            pltpu.VMEM(view.shape, data.dtype),
            pltpu.VMEM(shape, data.dtype),
            pltpu.SemaphoreType.DMA((chunks,)),
            pltpu.SemaphoreType.DMA((chunks,)),
        ],
        compiler_params=params(56),
    )(var_index[None], pattern.T, view)
    return out.reshape(devices, cols + 1, rows, width)


def pick_kernel(cols, shares, table_ref, *rest):
    out_ref, table, notes, digits, wanted, held, sem, sems = rest[-8:]
    devices = digits.shape[0]
    each = cols // shares
    tell = pltpu.make_async_copy(table_ref.at[:, pl.ds(cols, 1)], notes, sem.at[0])
    load = pltpu.make_async_copy(table_ref.at[:, pl.ds(0, cols + 1)], table, sem.at[1])
    tell.start()
    load.start()
    tell.wait()
    for u in range(devices):
        note = notes[u, 0].astype(F32)
        digits[u : u + 1, :] = (note[:1] * DIGIT + note[1:2]).astype(jnp.int32)
    move = pltpu.make_async_copy(digits, wanted, sem.at[2])
    move.start()
    move.wait()
    load.wait()
    flat = table.reshape((devices * (cols + 1),) + table.shape[2:])
    sent = []
    for s in range(shares):

        @pl.loop(0, devices, unroll=8)
        def _(d):
            for j in range(each):
                held[s, d, j] = flat[wanted[d, s * each + j]]

        copy = pltpu.make_async_copy(held.at[s], out_ref.at[pl.ds(s * devices, devices)], sems.at[s])
        copy.start()
        sent.append(copy)
    for copy in sent:
        copy.wait()


def pick(table, cols, shares, after):
    devices, _, rows, width = table.shape
    each = cols // shares
    return pl.pallas_call(
        functools.partial(pick_kernel, cols, shares),
        in_specs=[HBM] + [HBM] * len(after),
        out_specs=HBM,
        out_shape=jax.ShapeDtypeStruct((shares * devices, each, rows, width), table.dtype),
        scratch_shapes=[
            pltpu.VMEM((devices, cols + 1, rows, width), table.dtype),
            pltpu.VMEM((devices, 1, rows, width), table.dtype),
            pltpu.VMEM((devices, width), jnp.int32),
            pltpu.SMEM((devices, width), jnp.int32),
            pltpu.VMEM((shares, devices, each, rows, width), table.dtype),
            pltpu.SemaphoreType.DMA((3,)),
            pltpu.SemaphoreType.DMA((shares,)),
        ],
        compiler_params=params(56),
    )(table, *after)


def near_kernel(info_ref, own_ref, p1_ref, p2_ref, p3_ref, blocks_ref, gram_ref, turned_ref, start_ref, near):
    samp, rows, width = info_ref[0], own_ref.shape[0], own_ref.shape[1]
    for k, ref in enumerate((own_ref, p1_ref, p2_ref, p3_ref)):
        q = lax.rem(samp + 4 - k, 4)
        at = pl.multiple_of(q * rows, rows)
        x = ref[...]
        near[pl.ds(at, rows), :] = x
        turned_ref[0, :, pl.ds(at, rows)] = x.T
    gram_ref[0] = jnp.dot(turned_ref[0], near[...], preferred_element_type=F32)
    where_diag = info_ref[2 + pl.program_id(0)]
    start_ref[0, :width] = blocks_ref[0, where_diag]
    start_ref[0, width:] = blocks_ref[0, 1 - where_diag]


def near_panels(info, observed, received, blocks, each):
    rows, width = observed.shape[0], blocks.shape[-1]
    part = pl.BlockSpec((rows, width), lambda j, f: (0, j))
    return pl.pallas_call(
        near_kernel,
        grid_spec=pltpu.PrefetchScalarGridSpec(
            num_scalar_prefetch=1,
            grid=(each,),
            in_specs=[
                pl.BlockSpec((rows, width), lambda j, f: (0, f[1] + j)),
                part,
                part,
                part,
                pl.BlockSpec((1, 2, width, width), lambda j, f: (f[1] + j, 0, 0, 0)),
            ],
            out_specs=[
                pl.BlockSpec((1, width, width), lambda j, f: (j, 0, 0)),
                pl.BlockSpec((1, width, 4 * rows), lambda j, f: (j, 0, 0)),
                pl.BlockSpec((1, 2 * width, width), lambda j, f: (j, 0, 0)),
            ],
            scratch_shapes=[pltpu.VMEM((4 * rows, width), BF16)],
        ),
        out_shape=[
            jax.ShapeDtypeStruct((each, width, width), F32),
            jax.ShapeDtypeStruct((each, width, 4 * rows), BF16),
            jax.ShapeDtypeStruct((each, 2 * width, width), F32),
        ],
        compiler_params=params(56),
        cost_estimate=cost(1 << 20, 10 << 20),
    )(info, observed, *received, blocks)


def shrink(v, level):
    return jnp.where(v > level, v - level, jnp.where(v < -level, v + level, 0.0))


def split3(g):
    hi = g.astype(BF16)
    rest = g - hi.astype(F32)
    mid = rest.astype(BF16)
    return hi, mid, (rest - mid.astype(F32)).astype(BF16)


def steps_kernel(info_ref, far_ref, near_ref, turned_ref, start_ref, diag_ref, out0_ref, out1_ref, obj_ref):
    count, total_rows, width = far_ref.shape
    eye = lax.broadcasted_iota(jnp.int32, (width, width), 0) == lax.broadcasted_iota(jnp.int32, (width, width), 1)
    each = range(count)
    grams = []
    for c in each:
        far = far_ref[c]
        cross = jnp.dot(turned_ref[c], far, preferred_element_type=F32)
        own = lax.dot_general(far, far, (((0,), (0,)), ((), ())), preferred_element_type=F32)
        top = jnp.concatenate([near_ref[c], cross], axis=1)
        low = jnp.concatenate([cross.T, own], axis=1)
        grams.append(split3(jnp.concatenate([top, low], axis=0)))
    db = [jnp.where(eye, 0.0, start_ref[c, :width]) for c in each]
    ob = [start_ref[c, width:] for c in each]
    dv = [diag_ref[pl.ds(info_ref[1] + c, 1), :] for c in each]
    lane = lax.broadcasted_iota(jnp.int32, (1, width), 1)
    total = jnp.zeros((1, width), F32)
    for i in range(STEPS):
        w = [
            jnp.concatenate([jnp.where(eye, jnp.broadcast_to(dv[c], (width, width)), db[c]), ob[c]], axis=0).astype(BF16)
            for c in each
        ]
        g = [sum(jnp.dot(p, w[c], preferred_element_type=F32) for p in reversed(grams[c])) for c in each]
        part = jnp.zeros((1, width), F32)
        for c in each:
            fit = jnp.sum(w[c].astype(F32) * g[c], axis=0, keepdims=True) / (2.0 * total_rows)
            size = jnp.sum(jnp.abs(db[c]) + jnp.abs(ob[c]), axis=0, keepdims=True)
            part = part + (fit - jnp.log(dv[c]) + PENALTY * size)
        total = jnp.where(lane == i, jnp.sum(part, axis=1, keepdims=True), total)
        for c in each:
            gd, go = g[c][:width] / total_rows, g[c][width:] / total_rows
            along = jnp.sum(jnp.where(eye, gd, 0.0), axis=0, keepdims=True)
            db[c] = jnp.where(eye, 0.0, shrink(db[c] - STEP_LENGTH * gd, STEP_LENGTH * PENALTY))
            ob[c] = shrink(ob[c] - STEP_LENGTH * go, STEP_LENGTH * PENALTY)
            m = dv[c] - STEP_LENGTH * along
            dv[c] = 0.5 * (m + jnp.sqrt(m * m + 4.0 * STEP_LENGTH))
    obj_ref[...] = total
    for c in each:
        where_diag = info_ref[2 + c]
        full = jnp.where(eye, jnp.broadcast_to(dv[c], (width, width)), db[c])
        half = count // 2
        out_ref = out0_ref if c < half else out1_ref
        out_ref[c % half, where_diag] = full.astype(out_ref.dtype)
        out_ref[c % half, 1 - where_diag] = ob[c].astype(out_ref.dtype)


def iterate(info, far, near, turned, start, diag_rows):
    count, width = far.shape[0], far.shape[2]
    return pl.pallas_call(
        steps_kernel,
        in_specs=[pl.BlockSpec(memory_space=pltpu.SMEM)] + [VMEM] * 5,
        out_specs=[VMEM] * 3,
        out_shape=[
            jax.ShapeDtypeStruct((count // 2, 2, width, width), BF16),
            jax.ShapeDtypeStruct((count // 2, 2, width, width), BF16),
            jax.ShapeDtypeStruct((1, width), F32),
        ],
        compiler_params=params(24),
        cost_estimate=cost(count << 29, 4 << 20),
    )(info, far, near, turned, start, diag_rows)


def put(which_ref, out_ref, diag_ref, at, column, block):
    width = block.shape[-1]
    eye = lax.broadcasted_iota(jnp.int32, (width, width), 0) == lax.broadcasted_iota(jnp.int32, (width, width), 1)
    where_diag = which_ref[column]
    full = block[where_diag].astype(F32)
    diag_ref[pl.ds(column, 1), :] = jnp.sum(jnp.where(eye, full, 0.0), axis=0, keepdims=True)
    out_ref[at + (where_diag,)] = jnp.where(eye, 0.0, full)
    out_ref[at + (1 - where_diag,)] = block[1 - where_diag].astype(F32)


def first_places_kernel(samp_ref, which_ref, own0, own1, one0, one1, three0, three1, out_ref, diag_ref):
    @pl.when(pl.program_id(0) == 0)
    def _():
        diag_ref[...] = jnp.zeros_like(diag_ref)

    block = own0.shape[0]
    half = pl.num_programs(0) * block
    for k, refs in ((0, (own0, own1)), (1, (one0, one1)), (3, (three0, three1))):
        q = lax.rem(samp_ref[0] + 4 - k, 4)
        for h, ref in enumerate(refs):
            for c in range(block):
                put(which_ref, out_ref, diag_ref, (q, h, c), (q * 2 + h) * half + pl.program_id(0) * block + c, ref.at[c])


def last_places_kernel(samp_ref, which_ref, low_ref, high_ref, _, old_diag_ref, out_ref, diag_ref):
    @pl.when(pl.program_id(0) == 0)
    def _():
        diag_ref[...] = old_diag_ref[...]

    block = low_ref.shape[0]
    half = pl.num_programs(0) * block
    for h, ref in enumerate((low_ref, high_ref)):
        for c in range(block):
            column = (lax.rem(samp_ref[0] + 2, 4) * 2 + h) * half + pl.program_id(0) * block + c
            put(which_ref, out_ref, diag_ref, (0, h, c), column, ref.at[c])


def place_first(samp, which, own, one, three):
    half, tail = own[0].shape[0], own[0].shape[1:]
    zeros = (0,) * len(tail)
    block = 2
    part = pl.BlockSpec((block,) + tail, lambda j, f, w: (j,) + zeros)
    return pl.pallas_call(
        first_places_kernel,
        grid_spec=pltpu.PrefetchScalarGridSpec(
            num_scalar_prefetch=2,
            grid=(half // block,),
            in_specs=[part] * 6,
            out_specs=[
                pl.BlockSpec((4, 2, block) + tail, lambda j, f, w: (0, 0, j) + zeros),
                pl.BlockSpec((8 * half, tail[-1]), lambda j, f, w: (0, 0)),
            ],
        ),
        out_shape=[jax.ShapeDtypeStruct((4, 2, half) + tail, F32), jax.ShapeDtypeStruct((8 * half, tail[-1]), F32)],
        compiler_params=params(24),
        cost_estimate=cost(1 << 20, 6 << 20),
    )(samp[None], which, *own, *one, *three)


def place_last(samp, which, low, high, out, diagonal):
    half, tail = low.shape[0], low.shape[1:]
    zeros = (0,) * len(tail)
    block = 2
    shape = (4, 2, half) + tail
    part = pl.BlockSpec((block,) + tail, lambda j, f, w: (j,) + zeros)
    diag = pl.BlockSpec(diagonal.shape, lambda j, f, w: (0, 0))
    out, diagonal = pl.pallas_call(
        last_places_kernel,
        grid_spec=pltpu.PrefetchScalarGridSpec(
            num_scalar_prefetch=2,
            grid=(half // block,),
            in_specs=[part, part, ANY, diag],
            out_specs=[
                pl.BlockSpec((1, 2, block) + tail, lambda j, f, w: (lax.rem(f[0] + 2, 4), 0, j) + zeros),
                diag,
            ],
        ),
        out_shape=[
            jax.ShapeDtypeStruct(shape, F32),
            jax.ShapeDtypeStruct(diagonal.shape, F32),
        ],
        input_output_aliases={4: 0},
        compiler_params=params(16),
        cost_estimate=cost(1 << 20, 2 << 20),
    )(samp[None], which, low, high, out.reshape(shape), diagonal)
    return out.reshape((8 * half,) + tail), diagonal.reshape(-1)


def body(observed, blocks, diagonal, pattern):
    cols, _, width, _ = blocks.shape
    rows = observed.shape[0]
    devices = lax.axis_size(VAR)
    shares = lax.axis_size("samp")
    each = cols // shares
    total_rows = rows * shares
    samp = lax.axis_index("samp").astype(jnp.int32)
    var_index = lax.axis_index(VAR).astype(jnp.int32)

    pieces = cut(var_index, pattern, observed, devices, cols, width)
    panel = each * width
    received = [shift(lax.dynamic_slice_in_dim(observed, lax.rem(samp + k, shares) * panel, panel, 1), "samp", k) for k in (1, 2, 3)]
    table = lax.all_to_all(pieces, VAR, split_axis=0, concat_axis=0, tiled=True)
    start = samp * each
    columns = var_index * cols + jnp.arange(cols, dtype=jnp.int32)
    which = jnp.where(pattern[:, 0] == columns, 0, 1).astype(jnp.int32)
    info = jnp.concatenate([jnp.stack([samp, start]), lax.dynamic_slice_in_dim(which, start, each, 0)])
    near, turned, begin = near_panels(info, observed, received, blocks, each)
    outgoing = pick(table, cols, shares, (near, turned, begin))
    far = lax.all_to_all(outgoing, ALL, split_axis=0, concat_axis=0, tiled=True)

    diag_rows = diagonal.reshape(cols, width)
    far = far.transpose(1, 0, 2, 3).reshape(each, total_rows, width)
    *new, obj = iterate(info, far, near, turned, begin, diag_rows)
    one = [shift(x, "samp", 1) for x in new]
    three = [shift(x, "samp", 3) for x in new]
    two = [shift(one[0], "samp", 1), shift(three[1], "samp", 3)]
    terms = jnp.broadcast_to(obj[None], (shares * devices, 1, width))
    terms = lax.all_to_all(terms, ALL, split_axis=0, concat_axis=0, tiled=True)
    placed, diag = place_first(samp, which, new, one, three)
    terms, diag = lax.optimization_barrier((terms, diag))
    terms = jnp.sum(terms, axis=(0, 1))
    new_blocks, new_diagonal = place_last(samp, which, *two, placed, diag)
    return (new_blocks, new_diagonal, terms[:STEPS] / (cols * devices * width))


def solution(mesh):
    torus = Mesh(mesh.devices.reshape(mesh.shape["samp"], 4, 8, 2), ALL)
    placed = (P("samp", VAR), P(VAR, None, None, None), P(VAR), P(VAR, None))
    return jax.shard_map(
        body,
        mesh=torus,
        in_specs=placed,
        out_specs=(P(VAR, None, None, None), P(VAR), P()),
        check_vma=False,
    )
```
